256 devices in a mesh: replica: 8 (over x, core), mp: 32 (over y, z).
Axes of the slice: x: 4, y: 4, z: 8, core: 2. Of those that a mesh axis runs over, the one named last changes fastest.
Arguments:
- emb_table: float32 [131072, 256], P('mp'), may hold values from -3 to 3
- row_accum: float32 [131072], P('mp'), may hold values from 0.05 to 5
- row_grads: bfloat16 [1048576, 256], P(('replica', 'mp')), may hold values from -6 to 6
- owner_ids: int32 [1048576, 1], P(('replica', 'mp')), may hold values from 0 to 31; in each aligned block of 4096 rows (0 to 4095, 4096 to 8191, ...) at most 256 rows name the same one
- local_row: int32 [1048576], P(('replica', 'mp')), may hold values from 0 to 4095
Outputs:
- new_table: float32 [131072, 256], P('mp')
- new_accum: float32 [131072], P('mp')
The draws below stay inside these ranges and needn't reach their ends.
Inputs may be any that keep to these rules, and one draw needn't show every extreme that they name: `owner_ids`: among the lookups of one device, no owner is named more than 256 times, a bound that some block reaches.
All inputs are finite; a program needn't handle non-finite values.
Results may differ from the reference program's by a relative error of at most 0.0003.
Values may be sent and summed in bfloat16 or wider, within the bound.
No kernel may reach another device: no remote copies, remote signals or barrier semaphores. Data moves between devices by JAX's collectives and lax.ppermute only.
A program may use at most 64 MiB of HBM per device.

```python
import math
import jax
import jax.numpy as jnp
import numpy as np
from jax import lax

D = 256
SAMP = 4096
ROWS_DEV = 4096
CAP = 256
SAMPLES = 1048576
ROWS = 131072
N_REPLICA = 8
N_MP = 32


def touch_ends(result, own_key, low, largest):
    spot = [jax.random.randint(jax.random.fold_in(own_key, axis), (), 0, length) for axis, length in enumerate(result.shape)]
    longest = result.shape.index(max(result.shape))
    next_to = spot[:longest] + [(spot[longest] + 1) % result.shape[longest]] + spot[longest + 1:]
    return result.at[tuple(spot)].set(low).at[tuple(next_to)].set(largest)


def level_of(key, dims, cuts, low, high):
    factor_of = 1.0
    for position, blocks in cuts:
        draws = jax.random.uniform(jax.random.fold_in(jax.random.fold_in(key, 6), position), (blocks,), jnp.float32, low / len(cuts), high / len(cuts))
        factor_of = factor_of * jnp.repeat(jnp.exp(draws), dims[position] // blocks).reshape((-1,) + (1,) * (len(dims) - 1 - position))
    return factor_of


def rank_bounds(count, lean):
    portions = [(1 << 20) // math.isqrt(rank ** lean) + 1 for rank in range(1, count + 1)]
    deviation = 1 + sum(portions) // (1 << 30)
    return np.cumsum(np.array([max(1, weight // deviation) for weight in portions]))


def skewed_ids(stream_key, shape, count, skew):
    table = rank_bounds(count, skew)
    lot = jax.random.randint(jax.random.fold_in(stream_key, 1), shape, 0, int(table[count - 1]))
    grade = jnp.searchsorted(jnp.asarray(table, jnp.int32), lot, side="right")
    return jax.random.permutation(jax.random.fold_in(stream_key, 2), count)[grade].astype(jnp.int32)


def shared_out(own_key, own, number, rows, number_of, top, bound, slope):
    sequence = jax.random.permutation(own_key, number_of)
    crowded, ordinary = portions_of(number_of, rows * top, bound, slope, True), portions_of(number_of, rows * top, bound, slope, False)
    places = jnp.arange(number_of)

    def named(tallies, offset_by):
        used = int((tallies > 0).sum())
        fixed = max(1, used // 4)
        passed = fixed + (places - fixed + offset_by * (used - fixed)) % max(1, number_of - fixed)
        return jnp.zeros((number_of,), jnp.int32).at[sequence[jnp.where(places < fixed, places, passed)]].set(jnp.asarray(tallies, jnp.int32))

    tallies = jnp.where(number % 4 == 0, named(crowded, number // 4), named(ordinary, number - number // 4 - 1))
    mixed = jax.random.permutation(jax.random.fold_in(own, 3), number_of)
    source_of, receiver = mixed[0:number_of // 2 * 2:2], mixed[1:number_of // 2 * 2:2]
    room = jnp.minimum(tallies[source_of] - 1, bound - tallies[receiver]) // 2
    room = jnp.where((source_of == sequence[0]) | (receiver == sequence[0]) | (tallies[receiver] == 0), 0, jnp.maximum(room, 0))
    passed = jax.random.randint(jax.random.fold_in(own, 4), (number_of // 2,), 0, 1 << 20) % (room + 1)
    tallies = tallies.at[source_of].add(-passed).at[receiver].add(passed)
    members = jnp.searchsorted(jnp.cumsum(tallies), jnp.arange(rows * top), side="right").astype(jnp.int32)
    grid = members.reshape(top, rows).T
    grid = grid[jax.random.permutation(jax.random.fold_in(own, 1), rows)]
    offset_by = jax.random.randint(jax.random.fold_in(own, 2), (rows, 1), 0, top)
    return jnp.take_along_axis(grid, (jnp.arange(top)[None, :] + offset_by) % top, axis=1)


def portions_of(amount, total, bound, lean, full):
    portions = [(1 << 20) // math.isqrt(standing ** lean) + 1 for standing in range(1, amount + 1)]
    largest = bound if full else min(bound, max(-(-total // amount), total * portions[0] // sum(portions)))
    least = 1 if total - largest >= amount - 1 else 0
    given, surplus = [largest] + [least] * (amount - 1), total - largest - least * (amount - 1)
    while surplus > 0:
        movable = [i for i in range(1, amount) if given[i] < largest] or [i for i in range(1, amount) if given[i] < bound]
        whole, remaining = sum([portions[i] for i in movable]), surplus
        for i in movable:
            addition = min(bound - given[i], max(1, remaining * portions[i] // whole), surplus)
            given[i] = given[i] + addition
            surplus = surplus - addition
    return np.array(given)


def scatter_about(key, dims, spread, reach, split=(), held_as=jnp.bfloat16):
    factor_of = level_of(key, dims, split, -0.22, 0.18) if split else 1.0
    array = jax.random.normal(key, dims, jnp.float32) * spread * factor_of
    return jnp.minimum(jnp.maximum(array, -reach), reach).astype(held_as)


def setup_inputs(seed: int = 0) -> dict:
    key_list = jax.random.split(jax.random.key(seed), 6)
    emb_table = scatter_about(key_list[0], (ROWS, D), 0.5, 3.0, ((0, 32),), jnp.float32)
    row_accum = jnp.clip(jnp.exp(math.log(5.0) - 4.6051702 * jax.random.uniform(key_list[1], (ROWS,), jnp.float32) ** level_of(key_list[1], (ROWS,), ((0, 32),), -0.2, 0.2)), 0.05, 5.0)
    row_grads = scatter_about(key_list[2], (SAMPLES, D), 1.0, 6.0, ((0, 256),))
    owner_ids_keys = jax.random.split(jax.random.fold_in(key_list[3], 1), SAMPLES // SAMP)
    owner_ids_turns = jax.random.permutation(jax.random.fold_in(key_list[3], 3), SAMPLES // SAMP)
    owner_ids = jax.vmap(lambda own, number: shared_out(jax.random.fold_in(key_list[3], 2), own, number, SAMP, N_MP, 1, CAP, 2))(owner_ids_keys, owner_ids_turns).reshape((SAMPLES, 1))
    local_row = touch_ends(skewed_ids(key_list[4], (SAMPLES,), ROWS_DEV, 2), jax.random.fold_in(key_list[4], 3), 0, ROWS_DEV - 1).astype(jnp.int32)
    return dict(emb_table=emb_table, row_accum=row_accum, row_grads=row_grads, owner_ids=owner_ids, local_row=local_row)


learn_rate = 0.5

def reference(emb_table, row_accum, row_grads, owner_ids, local_row):
    global_rows = (owner_ids[:, 0] * ROWS_DEV + local_row).astype(jnp.int32)
    rows_grouped = global_rows.reshape(N_REPLICA, N_MP * SAMP)
    grads_grouped = row_grads.reshape(N_REPLICA, N_MP * SAMP, D)

    def one_replica(carry, inputs):
        delta_total, square_total = carry
        ids_here, grads_here = inputs
        summed = jax.ops.segment_sum(grads_here.astype(jnp.float32), ids_here, num_segments=ROWS)
        mean_square = lax.optimization_barrier(jnp.mean(summed * summed, axis=1))
        row_delta = -learn_rate * summed / jnp.sqrt(row_accum + mean_square)[:, None]
        return ((delta_total + row_delta, square_total + mean_square), None)
    start = (jnp.zeros((ROWS, D), jnp.float32), jnp.zeros((ROWS,), jnp.float32))
    totals, unused = lax.scan(one_replica, start, (rows_grouped, grads_grouped))
    delta_total, square_total = totals
    return (emb_table + delta_total / N_REPLICA, row_accum + square_total / N_REPLICA)
```

```python
import functools
import jax
import jax.numpy as jnp
from jax import lax
from jax.experimental import pallas as pl
from jax.experimental.pallas import tpu as pltpu
from jax.sharding import PartitionSpec as P

LANES = 128


def pack_kernel(owner_ref, row_ref, grads_ref, out_ref, x32, out32, slot_v, slot_s, sem, *, owners, cap, pad):
    nb = owner_ref.shape[0]
    n = nb * LANES
    sub = lax.broadcasted_iota(jnp.int32, (owners, LANES), 0)
    upper = (lax.broadcasted_iota(jnp.int32, (LANES, LANES), 0)
             < lax.broadcasted_iota(jnp.int32, (LANES, LANES), 1)).astype(jnp.bfloat16)
    cap_iota = lax.broadcasted_iota(jnp.int32, (cap, LANES), 0)
    carry = jnp.zeros((owners, 1), jnp.float32)
    tgt = jnp.zeros((2 * owners, cap), jnp.float32)
    for b in range(nb):
        own = owner_ref[b:b + 1, :]
        hit = sub == jnp.broadcast_to(own, (owners, LANES))
        hot = hit.astype(jnp.float32)
        before = jnp.dot(hot.astype(jnp.bfloat16), upper, preferred_element_type=jnp.float32)
        pos = jnp.sum(jnp.where(hit, before + carry, 0.0), axis=0, keepdims=True).astype(jnp.int32)
        carry = carry + jnp.sum(hot, axis=1, keepdims=True)
        slot_v[b:b + 1, :] = own * cap + pos
        code = row_ref[b:b + 1, :] + 1
        hi = (code >> 6).astype(jnp.float32)
        lo = (code & 63).astype(jnp.float32)
        lhs = jnp.concatenate([hot * hi, hot * lo], axis=0).astype(jnp.bfloat16)
        rhs = (cap_iota == jnp.broadcast_to(pos, (cap, LANES))).astype(jnp.float32).astype(jnp.bfloat16)
        tgt = tgt + lax.dot_general(lhs, rhs, (((1,), (1,)), ((), ())), preferred_element_type=jnp.float32)
    copy = pltpu.make_async_copy(slot_v, slot_s, sem)
    copy.start()
    tb = tgt.astype(jnp.bfloat16)
    parts = [tb[:owners, :LANES], tb[:owners, LANES:], tb[owners:, :LANES], tb[owners:, LANES:]]
    parts += [jnp.zeros((owners, LANES), jnp.bfloat16)] * (pad - 4)
    for k in range(pad):
        x = parts[k]
        for o in range(owners):
            out_ref[o, 2 * cap + k:2 * cap + k + 1, :] = x[o:o + 1, :]

    blk = 128

    @pl.loop(0, n // blk)
    def _(b):
        r = pl.multiple_of(b * blk, blk)
        g = grads_ref[pl.ds(r, blk), :].astype(jnp.float32)
        x32[pl.ds(2 * r, blk, stride=2), :] = g[:, :LANES]
        x32[pl.ds(2 * r + 1, blk, stride=2), :] = g[:, LANES:]

    copy.wait()

    @pl.loop(0, nb)
    def _(b):
        for j in range(LANES):
            s = slot_s[b, j]
            out32[pl.ds(2 * s, 2), :] = x32[pl.ds(2 * (b * LANES + j), 2), :]

    @pl.loop(0, owners)
    def _(o):
        out_ref[o, 0:2 * cap, :] = out32[pl.ds(pl.multiple_of(o * 2 * cap, 2 * cap), 2 * cap), :].astype(jnp.bfloat16)


def pack(owner, row, grads, owners, cap, pad=8):
    n = grads.shape[0]
    nb = n // LANES
    return pl.pallas_call(
        functools.partial(pack_kernel, owners=owners, cap=cap, pad=pad),
        out_shape=jax.ShapeDtypeStruct((owners, 2 * cap + pad, LANES), jnp.bfloat16),
        in_specs=[pl.BlockSpec(memory_space=pltpu.VMEM)] * 3,
        out_specs=pl.BlockSpec(memory_space=pltpu.VMEM),
        scratch_shapes=[
            pltpu.VMEM((2 * n, LANES), jnp.float32),
            pltpu.VMEM((2 * owners * cap, LANES), jnp.float32),
            pltpu.VMEM((nb, LANES), jnp.int32),
            pltpu.SMEM((nb, LANES), jnp.int32),
            pltpu.SemaphoreType.DMA,
        ],
        name="pack",
    )(owner, row, grads)


def reduce_kernel(recv_ref, acc_ref, delta_ref, ms_ref, xbuf, a0, a1, a2, a3, idx_v, idx_s, sem, *, cap, rows, lr):
    accs = [a0, a1, a2, a3]
    owners = recv_ref.shape[0]
    @pl.loop(0, owners)
    def _(o):
        t = recv_ref[o, 2 * cap:2 * cap + 8, :].astype(jnp.float32)
        code = (t[0:2] * 64.0 + t[2:4]).astype(jnp.int32)
        idx_v[pl.ds(2 * o, 2), :] = jnp.where(code == 0, 2 * rows, 2 * code - 2)
    copy = pltpu.make_async_copy(idx_v, idx_s, sem)
    copy.start()
    zb = 512
    @pl.loop(0, 2 * rows // zb)
    def _(b):
        for a in accs:
            a[pl.ds(pl.multiple_of(b * zb, zb), zb), :] = jnp.zeros((zb, LANES), jnp.float32)
    copy.wait()

    @pl.loop(0, owners)
    def _(o):
        xbuf[...] = recv_ref[o, 0:2 * cap, :].astype(jnp.float32)
        for h in range(2):
            @pl.loop(0, LANES // 16)
            def _(jb):
                for u in range(16):
                    j = jb * 16 + u
                    r = idx_s[2 * o + h, j]
                    a = accs[u % len(accs)]
                    a[pl.ds(r, 2), :] += xbuf[pl.ds(2 * (h * LANES + j), 2), :]

    rb = 128
    @pl.loop(0, rows // rb)
    def _(b):
        base = pl.multiple_of(b * 2 * rb, 2 * rb)
        lo = sum(a[pl.ds(base, rb, stride=2), :] for a in accs)
        hi = sum(a[pl.ds(base + 1, rb, stride=2), :] for a in accs)
        ms = (jnp.sum(lo * lo, axis=1, keepdims=True) + jnp.sum(hi * hi, axis=1, keepdims=True)) * (1.0 / 256.0)
        ms_b = jnp.broadcast_to(ms, (rb, LANES))
        acc_c = jnp.transpose(jnp.broadcast_to(acc_ref[pl.ds(b, 1), :], (rb, LANES)))
        coef = -lr / jnp.sqrt(acc_c + ms_b)
        r = pl.multiple_of(b * rb, rb)
        delta_ref[pl.ds(r, rb), 0:LANES] = lo * coef
        delta_ref[pl.ds(r, rb), LANES:2 * LANES] = hi * coef
        ms_ref[pl.ds(b, 1), :] = jnp.transpose(ms_b)[0:1, :]


def reduce(recv, acc2d, cap, lr):
    rows = acc2d.size
    return pl.pallas_call(
        functools.partial(reduce_kernel, cap=cap, rows=rows, lr=lr),
        out_shape=(jax.ShapeDtypeStruct((rows, 2 * LANES), jnp.float32),
                   jax.ShapeDtypeStruct(acc2d.shape, jnp.float32)),
        in_specs=[pl.BlockSpec(memory_space=pltpu.VMEM)] * 2,
        out_specs=(pl.BlockSpec(memory_space=pltpu.VMEM), pl.BlockSpec(memory_space=pltpu.VMEM)),
        scratch_shapes=[pltpu.VMEM((2 * cap, LANES), jnp.float32)]
        + [pltpu.VMEM((2 * rows + 8, LANES), jnp.float32)] * 4
        + [
            pltpu.VMEM((2 * recv.shape[0], LANES), jnp.int32),
            pltpu.SMEM((2 * recv.shape[0], LANES), jnp.int32),
            pltpu.SemaphoreType.DMA,
        ],
        name="reduce",
    )(recv, acc2d)


learn_rate = 0.5


def shards(emb_table, row_accum, row_grads, owner_ids, local_row):
    owners = lax.axis_size("mp")
    replicas = lax.axis_size("replica")
    n = row_grads.shape[0]
    rows = emb_table.shape[0]
    cap = 2 * n // owners
    own2d = owner_ids.reshape(n // LANES, LANES)
    row2d = local_row.reshape(n // LANES, LANES)
    outgoing = pack(own2d, row2d, row_grads, owners, cap)
    incoming = lax.all_to_all(outgoing, "mp", split_axis=0, concat_axis=0, tiled=True)
    delta, ms = reduce(incoming, row_accum.reshape(rows // LANES, LANES), cap, learn_rate)
    delta_total, square_total = lax.psum((delta, ms), "replica")
    return (emb_table + delta_total / replicas, row_accum + square_total.reshape(rows) / replicas)


def solution(mesh):
    return jax.shard_map(
        shards,
        mesh=mesh,
        in_specs=(
            P("mp", None),
            P("mp"),
            P(("replica", "mp"), None),
            P(("replica", "mp"), None),
            P(("replica", "mp")),
        ),
        out_specs=(P("mp", None), P("mp")),
        check_vma=False,
    )
```

```python
import functools
import jax
import jax.numpy as jnp
from jax import lax
from jax.experimental import pallas as pl
from jax.experimental.pallas import tpu as pltpu
from jax.sharding import PartitionSpec as P

LANES = 128


def pack_kernel(owner_ref, row_ref, grads_ref, out_ref, x32, out32, slot_v, slot_s, sem, *, owners, cap, pad):
    nb = owner_ref.shape[0]
    n = nb * LANES
    sub = lax.broadcasted_iota(jnp.int32, (owners, LANES), 0)
    upper = (lax.broadcasted_iota(jnp.int32, (LANES, LANES), 0)
             < lax.broadcasted_iota(jnp.int32, (LANES, LANES), 1)).astype(jnp.bfloat16)
    cap_iota = lax.broadcasted_iota(jnp.int32, (cap, LANES), 0)
    carry = jnp.zeros((owners, 1), jnp.float32)
    tgt = jnp.zeros((2 * owners, cap), jnp.float32)
    for b in range(nb):
        own = owner_ref[b:b + 1, :]
        hit = sub == jnp.broadcast_to(own, (owners, LANES))
        hot = hit.astype(jnp.float32)
        before = jnp.dot(hot.astype(jnp.bfloat16), upper, preferred_element_type=jnp.float32)
        pos = jnp.sum(jnp.where(hit, before + carry, 0.0), axis=0, keepdims=True).astype(jnp.int32)
        carry = carry + jnp.sum(hot, axis=1, keepdims=True)
        slot_v[b:b + 1, :] = own * cap + pos
        code = row_ref[b:b + 1, :] + 1
        hi = (code >> 6).astype(jnp.float32)
        lo = (code & 63).astype(jnp.float32)
        lhs = jnp.concatenate([hot * hi, hot * lo], axis=0).astype(jnp.bfloat16)
        rhs = (cap_iota == jnp.broadcast_to(pos, (cap, LANES))).astype(jnp.float32).astype(jnp.bfloat16)
        tgt = tgt + lax.dot_general(lhs, rhs, (((1,), (1,)), ((), ())), preferred_element_type=jnp.float32)
    copy = pltpu.make_async_copy(slot_v, slot_s, sem)
    copy.start()
    tb = tgt.astype(jnp.bfloat16)
    parts = [tb[:owners, :LANES], tb[:owners, LANES:], tb[owners:, :LANES], tb[owners:, LANES:]]
    parts += [jnp.zeros((owners, LANES), jnp.bfloat16)] * (pad - 4)
    for k in range(pad):
        x = parts[k]
        for o in range(owners):
            out_ref[o, 2 * cap + k:2 * cap + k + 1, :] = x[o:o + 1, :]

    blk = 128

    @pl.loop(0, n // blk)
    def _(b):
        r = pl.multiple_of(b * blk, blk)
        g = grads_ref[pl.ds(r, blk), :].astype(jnp.float32)
        x32[pl.ds(2 * r, blk, stride=2), :] = g[:, :LANES]
        x32[pl.ds(2 * r + 1, blk, stride=2), :] = g[:, LANES:]

    copy.wait()

    @pl.loop(0, nb)
    def _(b):
        for j in range(LANES):
            s = slot_s[b, j]
            out32[pl.ds(2 * s, 2), :] = x32[pl.ds(2 * (b * LANES + j), 2), :]

    @pl.loop(0, owners)
    def _(o):
        out_ref[o, 0:2 * cap, :] = out32[pl.ds(pl.multiple_of(o * 2 * cap, 2 * cap), 2 * cap), :].astype(jnp.bfloat16)


def pack(owner, row, grads, owners, cap, pad=8):
    n = grads.shape[0]
    nb = n // LANES
    return pl.pallas_call(
        functools.partial(pack_kernel, owners=owners, cap=cap, pad=pad),
        out_shape=jax.ShapeDtypeStruct((owners, 2 * cap + pad, LANES), jnp.bfloat16),
        in_specs=[pl.BlockSpec(memory_space=pltpu.VMEM)] * 3,
        out_specs=pl.BlockSpec(memory_space=pltpu.VMEM),
        scratch_shapes=[
            pltpu.VMEM((2 * n, LANES), jnp.float32),
            pltpu.VMEM((2 * owners * cap, LANES), jnp.float32),
            pltpu.VMEM((nb, LANES), jnp.int32),
            pltpu.SMEM((nb, LANES), jnp.int32),
            pltpu.SemaphoreType.DMA,
        ],
        name="pack",
    )(owner, row, grads)


def reduce_kernel(recv_ref, acc_ref, keep_ref, send_ref, xbuf, a0, a1, a2, a3, ms_v, idx_v, idx_s, sem, *, cap, rows, lr):
    accs = [a0, a1, a2, a3]
    owners = recv_ref.shape[0]
    @pl.loop(0, owners)
    def _(o):
        t = recv_ref[o, 2 * cap:2 * cap + 8, :].astype(jnp.float32)
        code = (t[0:2] * 64.0 + t[2:4]).astype(jnp.int32)
        idx_v[pl.ds(2 * o, 2), :] = jnp.where(code == 0, 2 * rows, 2 * code - 2)
    copy = pltpu.make_async_copy(idx_v, idx_s, sem)
    copy.start()
    zb = 512
    @pl.loop(0, 2 * rows // zb)
    def _(b):
        for a in accs:
            a[pl.ds(pl.multiple_of(b * zb, zb), zb), :] = jnp.zeros((zb, LANES), jnp.float32)
    copy.wait()

    @pl.loop(0, owners)
    def _(o):
        xbuf[...] = recv_ref[o, 0:2 * cap, :].astype(jnp.float32)
        for h in range(2):
            @pl.loop(0, LANES // 16)
            def _(jb):
                for u in range(16):
                    j = jb * 16 + u
                    r = idx_s[2 * o + h, j]
                    a = accs[u % len(accs)]
                    a[pl.ds(r, 2), :] += xbuf[pl.ds(2 * (h * LANES + j), 2), :]

    core = lax.rem(lax.axis_index("replica"), 2)
    half = rows // 2
    for ref, which in ((send_ref, 1 - core), (keep_ref, core)):

        @pl.loop(0, half // LANES)
        def _(b):
            block = which * (half // LANES) + b
            base = pl.multiple_of(block * 2 * LANES, 2 * LANES)
            lo = sum(a[pl.ds(base, LANES, stride=2), :] for a in accs)
            hi = sum(a[pl.ds(base + 1, LANES, stride=2), :] for a in accs)
            ms = (jnp.sum(lo * lo, axis=1, keepdims=True) + jnp.sum(hi * hi, axis=1, keepdims=True)) * (
                1.0 / (2 * LANES)
            )
            ms_b = jnp.broadcast_to(ms, (LANES, LANES))
            acc_c = jnp.transpose(jnp.broadcast_to(acc_ref[pl.ds(block, 1), :], (LANES, LANES)))
            coef = -lr / jnp.sqrt(acc_c + ms_b)
            r = pl.multiple_of(b * LANES, LANES)
            ref[pl.ds(r, LANES), 0:LANES] = lo * coef
            ref[pl.ds(r, LANES), LANES : 2 * LANES] = hi * coef
            ms_v[pl.ds(b, 1), :] = jnp.transpose(ms_b)[0:1, :]

        ref[half : half + half // LANES, 0:LANES] = ms_v[...]


def reduce(recv, acc2d, cap, lr):
    rows = acc2d.size
    return pl.pallas_call(
        functools.partial(reduce_kernel, cap=cap, rows=rows, lr=lr),
        out_shape=(jax.ShapeDtypeStruct((rows // 2 + rows // 2 // LANES, 2 * LANES), jnp.float32),) * 2,
        in_specs=[pl.BlockSpec(memory_space=pltpu.VMEM)] * 2,
        out_specs=(pl.BlockSpec(memory_space=pltpu.VMEM), pl.BlockSpec(memory_space=pltpu.VMEM)),
        scratch_shapes=[pltpu.VMEM((2 * cap, LANES), jnp.float32)]
        + [pltpu.VMEM((2 * rows + 8, LANES), jnp.float32)] * 4
        + [
            pltpu.VMEM((rows // 2 // LANES, LANES), jnp.float32),
            pltpu.VMEM((2 * recv.shape[0], LANES), jnp.int32),
            pltpu.SMEM((2 * recv.shape[0], LANES), jnp.int32),
            pltpu.SemaphoreType.DMA,
        ],
        name="reduce",
    )(recv, acc2d)


LOG_STEPS = 340.0
FINE = 1.3e7
FULL = 32767.0


def put_log(x):
    return jnp.floor(jnp.log(jnp.maximum(x, 1e-18)) * (LOG_STEPS / 0.6931471805599453))


def get_log(code):
    return jnp.exp(code * (0.6931471805599453 / LOG_STEPS))


def put_pair(x):
    hi = put_log(x)
    lo = jnp.round((x / get_log(hi) - 1.0) * FINE)
    return hi, jnp.clip(lo, -FULL, FULL)


def get_pair(hi, lo):
    return get_log(hi) * (1.0 + lo * (1.0 / FINE))


def to_i16(x):
    return x.astype(jnp.int32).astype(jnp.int16)


def from_i16(x):
    return x.astype(jnp.int32).astype(jnp.float32)


def encode(ref, tail, j, t, ms_row):
    top = jnp.max(jnp.abs(t), axis=1, keepdims=True)
    top_b = jnp.broadcast_to(top, (LANES, LANES))
    code = put_log(top_b) + 2.0
    inv = FULL / get_log(code)
    ref[j * LANES : (j + 1) * LANES, 0:LANES] = to_i16(jnp.clip(jnp.round(t[:, :LANES] * inv), -FULL, FULL))
    ref[j * LANES : (j + 1) * LANES, LANES : 2 * LANES] = to_i16(
        jnp.clip(jnp.round(t[:, LANES:] * inv), -FULL, FULL)
    )
    hi, lo = put_pair(ms_row)
    tail[j : j + 1, 0:LANES] = jnp.transpose(code)[0:1, :]
    tail[j : j + 1, LANES : 2 * LANES] = hi
    tail[4 + j : 5 + j, 0:LANES] = lo


def decode(ref, tail, j):
    code = jnp.transpose(jnp.broadcast_to(tail[j : j + 1, 0:LANES], (LANES, LANES)))
    step = get_log(code) * (1.0 / FULL)
    lo = from_i16(ref[j * LANES : (j + 1) * LANES, 0:LANES]) * step
    hi = from_i16(ref[j * LANES : (j + 1) * LANES, LANES : 2 * LANES]) * step
    ms = get_pair(tail[j : j + 1, LANES : 2 * LANES], tail[4 + j : 5 + j, 0:LANES])
    return lo, hi, ms


def pair_kernel(keep_ref, recv_ref, own_ref, q1, q2, q3, tail, ms_v):
    chip = lax.axis_index("replica") // 2
    part = own_ref.shape[0] - 4
    blocks = part // LANES
    half = 4 * part
    tail[...] = jnp.zeros_like(tail)
    ms_at = slice(half, half + half // LANES)
    ms_v[...] = keep_ref[ms_at, 0:LANES] + recv_ref[ms_at, 0:LANES]
    for shift, ref in ((2, q2), (1, q1), (3, q3), (0, own_ref)):
        quarter = lax.rem(chip + shift, 4)
        for j in range(blocks):
            b = quarter * blocks + j
            r = pl.multiple_of(b * LANES, LANES)
            t = keep_ref[pl.ds(r, LANES), :] + recv_ref[pl.ds(r, LANES), :]
            ms = ms_v[pl.ds(b, 1), :]
            if shift:
                encode(ref, tail, j, t, ms)
            else:
                ref[j * LANES : (j + 1) * LANES, :] = t
                ref[part + j : part + j + 1, 0:LANES] = ms
        if shift:
            ref[part : part + 16, :] = to_i16(tail[...])


def pair_sum(keep, recv, part):
    coded = jax.ShapeDtypeStruct((part + 16, 2 * LANES), jnp.int16)
    return pl.pallas_call(
        pair_kernel,
        out_shape=(jax.ShapeDtypeStruct((part + 4, 2 * LANES), jnp.float32), coded, coded, coded),
        in_specs=[pl.BlockSpec(memory_space=pltpu.VMEM)] * 2,
        out_specs=(pl.BlockSpec(memory_space=pltpu.VMEM),) * 4,
        scratch_shapes=[
            pltpu.VMEM((16, 2 * LANES), jnp.float32),
            pltpu.VMEM((4 * part // LANES, LANES), jnp.float32),
        ],
        name="pair_sum",
    )(keep, recv)


def chip_kernel(own_ref, r1, r2, r3, out_ref, tail, *, replicas):
    part = own_ref.shape[0] - 4
    tails = []
    for k, ref in enumerate((r1, r2, r3)):
        tail[16 * k : 16 * k + 16, :] = from_i16(ref[part : part + 16, :])
        tails.append(tail.at[16 * k : 16 * k + 16, :])
    last = tail.at[48:64, :]
    last[...] = jnp.zeros_like(last)
    for j in range(part // LANES):
        lo = own_ref[j * LANES : (j + 1) * LANES, 0:LANES]
        hi = own_ref[j * LANES : (j + 1) * LANES, LANES : 2 * LANES]
        ms = own_ref[part + j : part + j + 1, 0:LANES]
        for ref, t in zip((r1, r2, r3), tails):
            lo_k, hi_k, ms_k = decode(ref, t, j)
            lo, hi, ms = lo + lo_k, hi + hi_k, ms + ms_k
        both = jnp.concatenate([lo, hi], axis=1) * (1.0 / replicas)
        encode(out_ref, last, j, both, ms * (1.0 / replicas))
    out_ref[part : part + 16, :] = to_i16(last[...])


def chip_sum(own, r1, r2, r3, replicas):
    return pl.pallas_call(
        functools.partial(chip_kernel, replicas=replicas),
        out_shape=jax.ShapeDtypeStruct(r1.shape, jnp.int16),
        in_specs=[pl.BlockSpec(memory_space=pltpu.VMEM)] * 4,
        out_specs=pl.BlockSpec(memory_space=pltpu.VMEM),
        scratch_shapes=[pltpu.VMEM((64, 2 * LANES), jnp.float32)],
        name="chip_sum",
    )(own, r1, r2, r3)


def update_kernel(order_ref, emb_ref, acc_ref, *refs):
    pieces, (table_ref, accum_ref, tail) = refs[:-3], refs[-3:]
    part = pieces[0].shape[0] - 16
    blocks = part // LANES
    step = pl.program_id(0)
    for k, ref in enumerate(pieces):

        @pl.when(step == k)
        def _():
            tail[...] = from_i16(ref[part : part + 16, :])
            for j in range(blocks):
                lo, hi, ms = decode(ref, tail, j)
                rows = slice(j * LANES, (j + 1) * LANES)
                table_ref[rows, 0:LANES] = emb_ref[rows, 0:LANES] + lo
                table_ref[rows, LANES : 2 * LANES] = emb_ref[rows, LANES : 2 * LANES] + hi
                at = pl.ds(order_ref[k] * blocks + j, 1)
                accum_ref[at, :] = acc_ref[at, :] + ms


def update(order, emb, acc2d, pieces):
    part = pieces[0].shape[0] - 16
    whole = lambda x: pl.BlockSpec(x.shape, lambda s, order: (0, 0))
    moving = pl.BlockSpec((part, 2 * LANES), lambda s, order: (order[s], 0))
    return pl.pallas_call(
        update_kernel,
        out_shape=(jax.ShapeDtypeStruct(emb.shape, jnp.float32), jax.ShapeDtypeStruct(acc2d.shape, jnp.float32)),
        grid_spec=pltpu.PrefetchScalarGridSpec(
            num_scalar_prefetch=1,
            grid=(len(pieces),),
            in_specs=[moving, whole(acc2d)] + [whole(p) for p in pieces],
            out_specs=(moving, whole(acc2d)),
            scratch_shapes=[pltpu.VMEM((16, 2 * LANES), jnp.float32)],
        ),
        name="update",
    )(order, emb, acc2d, *pieces)


learn_rate = 0.5


def shards(emb_table, row_accum, row_grads, owner_ids, local_row):
    owners = lax.axis_size("mp")
    replicas = lax.axis_size("replica")
    n = row_grads.shape[0]
    rows = emb_table.shape[0]
    cap = 2 * n // owners
    own2d = owner_ids.reshape(n // LANES, LANES)
    row2d = local_row.reshape(n // LANES, LANES)
    acc2d = row_accum.reshape(rows // LANES, LANES)
    outgoing = pack(own2d, row2d, row_grads, owners, cap)
    incoming = lax.all_to_all(outgoing, "mp", split_axis=0, concat_axis=0, tiled=True)
    keep, send = reduce(incoming, acc2d, cap, learn_rate)

    def hop(v, chips):
        return lax.ppermute(v, "replica", [(k, (k + 2 * chips) % replicas) for k in range(replicas)])

    def swap(v):
        return lax.ppermute(v, "replica", [(k, k ^ 1) for k in range(replicas)])

    own, q1, q2, q3 = pair_sum(keep, swap(send), rows // replicas)
    mine = chip_sum(own, hop(q1, 1), hop(q2, 2), hop(q3, 3), replicas)
    here = [mine] + [hop(mine, s) for s in (1, 2, 3)]
    there = [swap(v) for v in here]
    me = lax.axis_index("replica")
    chip, core = me // 2, me % 2
    shift = jnp.arange(replicas // 2, dtype=jnp.int32)
    quarter = (chip - shift) % 4
    order = jnp.concatenate([core * 4 + quarter, (1 - core) * 4 + quarter]).astype(jnp.int32)
    table, accum = update(order, emb_table, acc2d, here + there)
    return table, accum.reshape(rows)


def solution(mesh):
    return jax.shard_map(
        shards,
        mesh=mesh,
        in_specs=(
            P("mp", None),
            P("mp"),
            P(("replica", "mp"), None),
            P(("replica", "mp"), None),
            P(("replica", "mp")),
        ),
        out_specs=(P("mp", None), P("mp")),
        check_vma=False,
    )
```

```python
import functools
import jax
import jax.numpy as jnp
from jax import lax
from jax.experimental import pallas as pl
from jax.experimental.pallas import tpu as pltpu
from jax.sharding import PartitionSpec as P

LANES = 128


def pack_kernel(
    owner_hbm, row_hbm, grads_hbm, out_ref, owner_ref, row_ref, grads_ref, x32, out32, slot_v, slot_s, sems, *, owners, cap, pad
):
    loads = [
        pltpu.make_async_copy(src, dst, sems.at[k])
        for k, (src, dst) in enumerate(((owner_hbm, owner_ref), (row_hbm, row_ref), (grads_hbm, grads_ref)))
    ]
    for load in loads:
        load.start()
    nb = owner_ref.shape[0]
    n = nb * LANES
    sub = lax.broadcasted_iota(jnp.int32, (owners, LANES), 0)
    upper = (lax.broadcasted_iota(jnp.int32, (LANES, LANES), 0)
             < lax.broadcasted_iota(jnp.int32, (LANES, LANES), 1)).astype(jnp.bfloat16)
    cap_iota = lax.broadcasted_iota(jnp.int32, (cap, LANES), 0)
    loads[0].wait()
    loads[1].wait()
    carry = jnp.zeros((owners, 1), jnp.float32)
    tgt = jnp.zeros((2 * owners, cap), jnp.float32)
    for b in range(nb):
        own = owner_ref[b:b + 1, :]
        hit = sub == jnp.broadcast_to(own, (owners, LANES))
        hot = hit.astype(jnp.float32)
        before = jnp.dot(hot.astype(jnp.bfloat16), upper, preferred_element_type=jnp.float32)
        pos = jnp.sum(jnp.where(hit, before + carry, 0.0), axis=0, keepdims=True).astype(jnp.int32)
        carry = carry + jnp.sum(hot, axis=1, keepdims=True)
        slot_v[b:b + 1, :] = 2 * (own * cap + pos)
        code = row_ref[b:b + 1, :] + 1
        hi = (code >> 6).astype(jnp.float32)
        lo = (code & 63).astype(jnp.float32)
        lhs = jnp.concatenate([hot * hi, hot * lo], axis=0).astype(jnp.bfloat16)
        rhs = (cap_iota == jnp.broadcast_to(pos, (cap, LANES))).astype(jnp.float32).astype(jnp.bfloat16)
        tgt = tgt + lax.dot_general(lhs, rhs, (((1,), (1,)), ((), ())), preferred_element_type=jnp.float32)
    copy = pltpu.make_async_copy(slot_v, slot_s, sems.at[3])
    copy.start()
    tb = tgt.astype(jnp.bfloat16)
    parts = [tb[:owners, :LANES], tb[:owners, LANES:], tb[owners:, :LANES], tb[owners:, LANES:]]
    parts += [jnp.zeros((owners, LANES), jnp.bfloat16)] * (pad - 4)
    for k in range(pad):
        x = parts[k]
        for o in range(owners):
            out_ref[o, 2 * cap + k:2 * cap + k + 1, :] = x[o:o + 1, :]

    blk = 128
    loads[2].wait()

    @pl.loop(0, n // blk)
    def _(b):
        r = pl.multiple_of(b * blk, blk)
        g = grads_ref[pl.ds(r, blk), :].astype(jnp.float32)
        x32[pl.ds(2 * r, blk, stride=2), :] = g[:, :LANES]
        x32[pl.ds(2 * r + 1, blk, stride=2), :] = g[:, LANES:]

    copy.wait()

    @pl.loop(0, nb)
    def _(b):
        for j in range(LANES):
            s = slot_s[b, j]
            out32[pl.ds(s, 2), :] = x32[pl.ds(2 * (b * LANES + j), 2), :]

    @pl.loop(0, owners)
    def _(o):
        out_ref[o, 0:2 * cap, :] = out32[pl.ds(pl.multiple_of(o * 2 * cap, 2 * cap), 2 * cap), :].astype(jnp.bfloat16)


def pack(owner, row, grads, owners, cap, pad=8):
    n = grads.shape[0]
    nb = n // LANES
    return pl.pallas_call(
        functools.partial(pack_kernel, owners=owners, cap=cap, pad=pad),
        out_shape=jax.ShapeDtypeStruct((owners, 2 * cap + pad, LANES), jnp.bfloat16),
        in_specs=[pl.BlockSpec(memory_space=pltpu.HBM)] * 3,
        out_specs=pl.BlockSpec(memory_space=pltpu.VMEM),
        scratch_shapes=[
            pltpu.VMEM((nb, LANES), jnp.int32),
            pltpu.VMEM((nb, LANES), jnp.int32),
            pltpu.VMEM((n, 2 * LANES), jnp.bfloat16),
            pltpu.VMEM((2 * n, LANES), jnp.float32),
            pltpu.VMEM((2 * owners * cap, LANES), jnp.float32),
            pltpu.VMEM((nb, LANES), jnp.int32),
            pltpu.SMEM((nb, LANES), jnp.int32),
            pltpu.SemaphoreType.DMA((4,)),
        ],
        compiler_params=pltpu.CompilerParams(vmem_limit_bytes=24 << 20),
        name="pack",
    )(*[pltpu.with_memory_space_constraint(x, pltpu.HBM) for x in (owner, row, grads)])


def reduce_kernel(recv_ref, acc_ref, keep_ref, send_ref, xbuf, a0, a1, a2, a3, ms_v, idx_v, idx_s, sem, *, cap, rows, lr):
    accs = [a0, a1, a2, a3]
    owners = recv_ref.shape[0]
    @pl.loop(0, owners)
    def _(o):
        t = recv_ref[o, 2 * cap:2 * cap + 8, :].astype(jnp.float32)
        code = (t[0:2] * 64.0 + t[2:4]).astype(jnp.int32)
        idx_v[pl.ds(2 * o, 2), :] = jnp.where(code == 0, 2 * rows, 2 * code - 2)
    copy = pltpu.make_async_copy(idx_v, idx_s, sem)
    copy.start()
    zb = 512
    @pl.loop(0, 2 * rows // zb)
    def _(b):
        for a in accs:
            a[pl.ds(pl.multiple_of(b * zb, zb), zb), :] = jnp.zeros((zb, LANES), jnp.float32)
    copy.wait()

    @pl.loop(0, owners)
    def _(o):
        xbuf[...] = recv_ref[o, 0:2 * cap, :].astype(jnp.float32)
        for h in range(2):
            for j in range(LANES):
                at = pl.ds(idx_s[2 * o + h, j], 2)
                accs[j % 4][at, :] += xbuf[2 * (h * LANES + j) : 2 * (h * LANES + j) + 2, :]

    core = lax.rem(lax.axis_index("replica"), 2)
    half = rows // 2
    for ref, which in ((send_ref, 1 - core), (keep_ref, core)):

        @pl.loop(0, half // LANES)
        def _(b):
            block = which * (half // LANES) + b
            base = pl.multiple_of(block * 2 * LANES, 2 * LANES)
            lo, hi = [
                (a0[at, :] + a1[at, :]) + (a2[at, :] + a3[at, :])
                for at in (pl.ds(base, LANES, stride=2), pl.ds(base + 1, LANES, stride=2))
            ]
            total = jnp.sum(lo * lo + hi * hi, axis=1, keepdims=True)
            ms = jnp.transpose(jnp.broadcast_to(total, (LANES, LANES)))[0:1, :] * (1.0 / (2 * LANES))
            ms_v[pl.ds(b, 1), :] = ms
            coef = -lr / jnp.sqrt(acc_ref[pl.ds(block, 1), :] + ms)
            coef = jnp.transpose(jnp.broadcast_to(coef, (LANES, LANES)))
            r = pl.multiple_of(b * LANES, LANES)
            ref[pl.ds(r, LANES), 0:LANES] = lo * coef
            ref[pl.ds(r, LANES), LANES : 2 * LANES] = hi * coef

        ref[half : half + half // LANES, 0:LANES] = ms_v[...]


def reduce(recv, acc2d, cap, lr):
    rows = acc2d.size
    return pl.pallas_call(
        functools.partial(reduce_kernel, cap=cap, rows=rows, lr=lr),
        out_shape=(jax.ShapeDtypeStruct((rows // 2 + rows // 2 // LANES, 2 * LANES), jnp.float32),) * 2,
        in_specs=[pl.BlockSpec(memory_space=pltpu.VMEM)] * 2,
        out_specs=(pl.BlockSpec(memory_space=pltpu.VMEM), pl.BlockSpec(memory_space=pltpu.VMEM)),
        scratch_shapes=[pltpu.VMEM((2 * cap, LANES), jnp.float32)]
        + [pltpu.VMEM((2 * rows + 8, LANES), jnp.float32)] * 4
        + [
            pltpu.VMEM((rows // 2 // LANES, LANES), jnp.float32),
            pltpu.VMEM((2 * recv.shape[0], LANES), jnp.int32),
            pltpu.SMEM((2 * recv.shape[0], LANES), jnp.int32),
            pltpu.SemaphoreType.DMA,
        ],
        compiler_params=pltpu.CompilerParams(vmem_limit_bytes=32 << 20),
        name="reduce",
    )(recv, acc2d)


LOG_STEPS = 340.0
FINE = 1.3e7
FULL = 32767.0


def put_log(x):
    return jnp.floor(jnp.log(jnp.maximum(x, 1e-18)) * (LOG_STEPS / 0.6931471805599453))


def get_log(code):
    return jnp.exp(code * (0.6931471805599453 / LOG_STEPS))


def put_pair(x):
    hi = put_log(x)
    lo = jnp.round((x / get_log(hi) - 1.0) * FINE)
    return hi, jnp.clip(lo, -FULL, FULL)


def get_pair(hi, lo):
    return get_log(hi) * (1.0 + lo * (1.0 / FINE))


def to_i16(x):
    return x.astype(jnp.int32).astype(jnp.int16)


def from_i16(x):
    return x.astype(jnp.int32).astype(jnp.float32)


def encode(ref, tail, j, t, ms_row):
    top = jnp.max(jnp.abs(t), axis=1, keepdims=True)
    top_b = jnp.broadcast_to(top, (LANES, LANES))
    code = put_log(top_b) + 2.0
    inv = FULL / get_log(code)
    ref[j * LANES : (j + 1) * LANES, 0:LANES] = to_i16(jnp.clip(jnp.round(t[:, :LANES] * inv), -FULL, FULL))
    ref[j * LANES : (j + 1) * LANES, LANES : 2 * LANES] = to_i16(
        jnp.clip(jnp.round(t[:, LANES:] * inv), -FULL, FULL)
    )
    hi, lo = put_pair(ms_row)
    tail[j : j + 1, 0:LANES] = jnp.transpose(code)[0:1, :]
    tail[j : j + 1, LANES : 2 * LANES] = hi
    tail[4 + j : 5 + j, 0:LANES] = lo


def decode(ref, tail, j):
    code = jnp.transpose(jnp.broadcast_to(tail[j : j + 1, 0:LANES], (LANES, LANES)))
    step = get_log(code) * (1.0 / FULL)
    lo = from_i16(ref[j * LANES : (j + 1) * LANES, 0:LANES]) * step
    hi = from_i16(ref[j * LANES : (j + 1) * LANES, LANES : 2 * LANES]) * step
    ms = get_pair(tail[j : j + 1, LANES : 2 * LANES], tail[4 + j : 5 + j, 0:LANES])
    return lo, hi, ms


def pair_kernel(keep_ref, recv_ref, own_ref, q1, q2, q3, tail, ms_v):
    chip = lax.axis_index("replica") // 2
    part = own_ref.shape[0] - 4
    blocks = part // LANES
    half = 4 * part
    tail[...] = jnp.zeros_like(tail)
    ms_at = slice(half, half + half // LANES)
    ms_v[...] = keep_ref[ms_at, 0:LANES] + recv_ref[ms_at, 0:LANES]
    for shift, ref in ((2, q2), (1, q1), (3, q3), (0, own_ref)):
        quarter = lax.rem(chip + shift, 4)
        for j in range(blocks):
            b = quarter * blocks + j
            r = pl.multiple_of(b * LANES, LANES)
            t = keep_ref[pl.ds(r, LANES), :] + recv_ref[pl.ds(r, LANES), :]
            ms = ms_v[pl.ds(b, 1), :]
            if shift:
                encode(ref, tail, j, t, ms)
            else:
                ref[j * LANES : (j + 1) * LANES, :] = t
                ref[part + j : part + j + 1, 0:LANES] = ms
        if shift:
            ref[part : part + 16, :] = to_i16(tail[...])


def pair_sum(keep, recv, part):
    coded = jax.ShapeDtypeStruct((part + 16, 2 * LANES), jnp.int16)
    return pl.pallas_call(
        pair_kernel,
        out_shape=(jax.ShapeDtypeStruct((part + 4, 2 * LANES), jnp.float32), coded, coded, coded),
        in_specs=[pl.BlockSpec(memory_space=pltpu.VMEM)] * 2,
        out_specs=(pl.BlockSpec(memory_space=pltpu.VMEM),) * 4,
        scratch_shapes=[
            pltpu.VMEM((16, 2 * LANES), jnp.float32),
            pltpu.VMEM((4 * part // LANES, LANES), jnp.float32),
        ],
        compiler_params=pltpu.CompilerParams(vmem_limit_bytes=12 << 20),
        name="pair_sum",
    )(keep, recv)


def chip_kernel(own_ref, r1, r2, r3, out_ref, tail, *, replicas):
    part = own_ref.shape[0] - 4
    tails = []
    for k, ref in enumerate((r1, r2, r3)):
        tail[16 * k : 16 * k + 16, :] = from_i16(ref[part : part + 16, :])
        tails.append(tail.at[16 * k : 16 * k + 16, :])
    last = tail.at[48:64, :]
    last[...] = jnp.zeros_like(last)
    for j in range(part // LANES):
        lo = own_ref[j * LANES : (j + 1) * LANES, 0:LANES]
        hi = own_ref[j * LANES : (j + 1) * LANES, LANES : 2 * LANES]
        ms = own_ref[part + j : part + j + 1, 0:LANES]
        for ref, t in zip((r1, r2, r3), tails):
            lo_k, hi_k, ms_k = decode(ref, t, j)
            lo, hi, ms = lo + lo_k, hi + hi_k, ms + ms_k
        both = jnp.concatenate([lo, hi], axis=1) * (1.0 / replicas)
        encode(out_ref, last, j, both, ms * (1.0 / replicas))
    out_ref[part : part + 16, :] = to_i16(last[...])


def chip_sum(own, r1, r2, r3, replicas):
    return pl.pallas_call(
        functools.partial(chip_kernel, replicas=replicas),
        out_shape=jax.ShapeDtypeStruct(r1.shape, jnp.int16),
        in_specs=[pl.BlockSpec(memory_space=pltpu.VMEM)] * 4,
        out_specs=pl.BlockSpec(memory_space=pltpu.VMEM),
        scratch_shapes=[pltpu.VMEM((64, 2 * LANES), jnp.float32)],
        compiler_params=pltpu.CompilerParams(vmem_limit_bytes=12 << 20),
        name="chip_sum",
    )(own, r1, r2, r3)


def update_kernel(emb_hbm, acc_ref, *refs, pieces):
    codes, (table_hbm, accum_ref, buf, tail, in_sems, out_sems) = refs[:pieces], refs[pieces:]
    part = buf.shape[1]
    blocks = part // LANES
    me = lax.axis_index("replica")
    chip, core = me // 2, lax.rem(me, 2)
    places = [
        (core if k < pieces // 2 else 1 - core) * (pieces // 2) + lax.rem(chip + pieces - k, pieces // 2)
        for k in range(pieces)
    ]
    spans = [pl.ds(pl.multiple_of(place * part, part), part) for place in places]
    loads = [pltpu.make_async_copy(emb_hbm.at[span], buf.at[k], in_sems.at[k]) for k, span in enumerate(spans)]
    stores = [pltpu.make_async_copy(buf.at[k], table_hbm.at[span], out_sems.at[k]) for k, span in enumerate(spans)]
    for load in loads:
        load.start()
    for k, ref in enumerate(codes):
        tail[...] = from_i16(ref[part : part + 16, :])
        loads[k].wait()
        for j in range(blocks):
            lo, hi, ms = decode(ref, tail, j)
            rows = slice(j * LANES, (j + 1) * LANES)
            buf[k, rows, 0:LANES] += lo
            buf[k, rows, LANES : 2 * LANES] += hi
            at = pl.ds(places[k] * blocks + j, 1)
            accum_ref[at, :] = acc_ref[at, :] + ms
        stores[k].start()
    for store in stores:
        store.wait()


def update(emb, acc2d, codes):
    part = codes[0].shape[0] - 16
    pieces = len(codes)
    return pl.pallas_call(
        functools.partial(update_kernel, pieces=pieces),
        out_shape=(jax.ShapeDtypeStruct(emb.shape, jnp.float32), jax.ShapeDtypeStruct(acc2d.shape, jnp.float32)),
        in_specs=[pl.BlockSpec(memory_space=pltpu.HBM)] + [pl.BlockSpec(memory_space=pltpu.VMEM)] * (1 + pieces),
        out_specs=(pl.BlockSpec(memory_space=pltpu.HBM), pl.BlockSpec(memory_space=pltpu.VMEM)),
        scratch_shapes=[
            pltpu.VMEM((pieces, part, 2 * LANES), jnp.float32),
            pltpu.VMEM((16, 2 * LANES), jnp.float32),
            pltpu.SemaphoreType.DMA((pieces,)),
            pltpu.SemaphoreType.DMA((pieces,)),
        ],
        compiler_params=pltpu.CompilerParams(vmem_limit_bytes=20 << 20),
        name="update",
    )(pltpu.with_memory_space_constraint(emb, pltpu.HBM), acc2d, *codes)


learn_rate = 0.5


def shards(emb_table, row_accum, row_grads, owner_ids, local_row):
    owners = lax.axis_size("mp")
    replicas = lax.axis_size("replica")
    n = row_grads.shape[0]
    rows = emb_table.shape[0]
    cap = 2 * n // owners
    own2d = owner_ids.reshape(n // LANES, LANES)
    row2d = local_row.reshape(n // LANES, LANES)
    acc2d = row_accum.reshape(rows // LANES, LANES)
    outgoing = pack(own2d, row2d, row_grads, owners, cap)
    incoming = lax.all_to_all(outgoing, "mp", split_axis=0, concat_axis=0, tiled=True)
    keep, send = reduce(incoming, acc2d, cap, learn_rate)

    def hop(v, chips):
        return lax.ppermute(v, "replica", [(k, (k + 2 * chips) % replicas) for k in range(replicas)])

    def swap(v):
        return lax.ppermute(v, "replica", [(k, k ^ 1) for k in range(replicas)])

    own, q1, q2, q3 = pair_sum(keep, swap(send), rows // replicas)
    mine = chip_sum(own, hop(q1, 1), hop(q2, 2), hop(q3, 3), replicas)
    here = [mine] + [hop(mine, s) for s in (1, 2, 3)]
    there = [swap(v) for v in here]
    table, accum = update(emb_table, acc2d, here + there)
    return table, accum.reshape(rows)


def solution(mesh):
    return jax.shard_map(
        shards,
        mesh=mesh,
        in_specs=(
            P("mp", None),
            P("mp"),
            P(("replica", "mp"), None),
            P(("replica", "mp"), None),
            P(("replica", "mp")),
        ),
        out_specs=(P("mp", None), P("mp")),
        check_vma=False,
    )
```

```python
import functools
import jax
import jax.numpy as jnp
from jax import lax
from jax.experimental import pallas as pl
from jax.experimental.pallas import tpu as pltpu
from jax.sharding import PartitionSpec as P

LANES = 128


def pack_kernel(
    owner_hbm, row_hbm, grads_hbm, out_ref, owner_ref, row_ref, grads_ref, x32, out32, slot_v, slot_s, sems, *, owners, cap, pad
):
    loads = [
        pltpu.make_async_copy(src, dst, sems.at[k])
        for k, (src, dst) in enumerate(((owner_hbm, owner_ref), (row_hbm, row_ref), (grads_hbm, grads_ref)))
    ]
    for load in loads:
        load.start()
    nb = owner_ref.shape[0]
    n = nb * LANES
    sub = lax.broadcasted_iota(jnp.int32, (owners, LANES), 0)
    upper = (lax.broadcasted_iota(jnp.int32, (LANES, LANES), 0)
             < lax.broadcasted_iota(jnp.int32, (LANES, LANES), 1)).astype(jnp.bfloat16)
    cap_iota = lax.broadcasted_iota(jnp.int32, (cap, LANES), 0)
    loads[0].wait()
    loads[1].wait()
    carry = jnp.zeros((owners, 1), jnp.float32)
    tgt = jnp.zeros((2 * owners, cap), jnp.float32)
    for b in range(nb):
        own = owner_ref[b:b + 1, :]
        hit = sub == jnp.broadcast_to(own, (owners, LANES))
        hot = hit.astype(jnp.float32)
        before = jnp.dot(hot.astype(jnp.bfloat16), upper, preferred_element_type=jnp.float32)
        pos = jnp.sum(jnp.where(hit, before + carry, 0.0), axis=0, keepdims=True).astype(jnp.int32)
        carry = carry + jnp.sum(hot, axis=1, keepdims=True)
        slot_v[b:b + 1, :] = 2 * (own * cap + pos)
        code = row_ref[b:b + 1, :] + 1
        hi = (code >> 6).astype(jnp.float32)
        lo = (code & 63).astype(jnp.float32)
        lhs = jnp.concatenate([hot * hi, hot * lo], axis=0).astype(jnp.bfloat16)
        rhs = (cap_iota == jnp.broadcast_to(pos, (cap, LANES))).astype(jnp.float32).astype(jnp.bfloat16)
        tgt = tgt + lax.dot_general(lhs, rhs, (((1,), (1,)), ((), ())), preferred_element_type=jnp.float32)
    copy = pltpu.make_async_copy(slot_v, slot_s, sems.at[3])
    copy.start()
    tb = tgt.astype(jnp.bfloat16)
    parts = [tb[:owners, :LANES], tb[:owners, LANES:], tb[owners:, :LANES], tb[owners:, LANES:]]
    parts += [jnp.zeros((owners, LANES), jnp.bfloat16)] * (pad - 4)
    for k in range(pad):
        x = parts[k]
        for o in range(owners):
            out_ref[o, 2 * cap + k:2 * cap + k + 1, :] = x[o:o + 1, :]

    blk = 128
    loads[2].wait()

    @pl.loop(0, n // blk)
    def _(b):
        r = pl.multiple_of(b * blk, blk)
        g = grads_ref[pl.ds(r, blk), :].astype(jnp.float32)
        x32[pl.ds(2 * r, blk, stride=2), :] = g[:, :LANES]
        x32[pl.ds(2 * r + 1, blk, stride=2), :] = g[:, LANES:]

    copy.wait()

    @pl.loop(0, nb)
    def _(b):
        for j in range(LANES):
            s = slot_s[b, j]
            out32[pl.ds(s, 2), :] = x32[pl.ds(2 * (b * LANES + j), 2), :]

    @pl.loop(0, owners)
    def _(o):
        out_ref[o, 0:2 * cap, :] = out32[pl.ds(pl.multiple_of(o * 2 * cap, 2 * cap), 2 * cap), :].astype(jnp.bfloat16)


def pack(owner, row, grads, owners, cap, pad=8):
    n = grads.shape[0]
    nb = n // LANES
    return pl.pallas_call(
        functools.partial(pack_kernel, owners=owners, cap=cap, pad=pad),
        out_shape=jax.ShapeDtypeStruct((owners, 2 * cap + pad, LANES), jnp.bfloat16),
        in_specs=[pl.BlockSpec(memory_space=pltpu.HBM)] * 3,
        out_specs=pl.BlockSpec(memory_space=pltpu.VMEM),
        scratch_shapes=[
            pltpu.VMEM((nb, LANES), jnp.int32),
            pltpu.VMEM((nb, LANES), jnp.int32),
            pltpu.VMEM((n, 2 * LANES), jnp.bfloat16),
            pltpu.VMEM((2 * n, LANES), jnp.float32),
            pltpu.VMEM((2 * owners * cap, LANES), jnp.float32),
            pltpu.VMEM((nb, LANES), jnp.int32),
            pltpu.SMEM((nb, LANES), jnp.int32),
            pltpu.SemaphoreType.DMA((4,)),
        ],
        compiler_params=pltpu.CompilerParams(vmem_limit_bytes=24 << 20),
        name="pack",
    )(*[pltpu.with_memory_space_constraint(x, pltpu.HBM) for x in (owner, row, grads)])


def reduce_kernel(recv_ref, acc_ref, keep_ref, send_ref, xbuf, a0, a1, a2, a3, ms_v, idx_v, idx_s, sem, *, cap, rows, lr):
    accs = [a0, a1, a2, a3]
    owners = recv_ref.shape[0]
    @pl.loop(0, owners)
    def _(o):
        t = recv_ref[o, 2 * cap:2 * cap + 8, :].astype(jnp.float32)
        code = (t[0:2] * 64.0 + t[2:4]).astype(jnp.int32)
        idx_v[pl.ds(2 * o, 2), :] = jnp.where(code == 0, 2 * rows, 2 * code - 2)
    copy = pltpu.make_async_copy(idx_v, idx_s, sem)
    copy.start()
    zb = 512
    @pl.loop(0, 2 * rows // zb)
    def _(b):
        for a in accs:
            a[pl.ds(pl.multiple_of(b * zb, zb), zb), :] = jnp.zeros((zb, LANES), jnp.float32)
    copy.wait()

    @pl.loop(0, owners)
    def _(o):
        xbuf[...] = recv_ref[o, 0:2 * cap, :].astype(jnp.float32)
        for h in range(2):
            for j in range(LANES):
                at = pl.ds(idx_s[2 * o + h, j], 2)
                accs[j % 4][at, :] += xbuf[2 * (h * LANES + j) : 2 * (h * LANES + j) + 2, :]

    core = lax.rem(lax.axis_index("replica"), 2)
    half = rows // 2
    for ref, which in ((send_ref, 1 - core), (keep_ref, core)):
        for b in range(half // LANES):
            block = which * (half // LANES) + b
            base = pl.multiple_of(block * 2 * LANES, 2 * LANES)
            lo, hi = [
                (a0[at, :] + a1[at, :]) + (a2[at, :] + a3[at, :])
                for at in (pl.ds(base, LANES, stride=2), pl.ds(base + 1, LANES, stride=2))
            ]
            total = jnp.sum(lo * lo + hi * hi, axis=1, keepdims=True)
            ms = jnp.transpose(jnp.broadcast_to(total, (LANES, LANES)))[0:1, :] * (1.0 / (2 * LANES))
            ms_v[b : b + 1, :] = ms
            coef = -lr / jnp.sqrt(acc_ref[pl.ds(block, 1), :] + ms)
            coef = jnp.transpose(jnp.broadcast_to(coef, (LANES, LANES)))
            ref[b * LANES : (b + 1) * LANES, 0:LANES] = lo * coef
            ref[b * LANES : (b + 1) * LANES, LANES : 2 * LANES] = hi * coef

        ref[half : half + half // LANES, 0:LANES] = ms_v[...]


def reduce(recv, acc2d, cap, lr):
    rows = acc2d.size
    return pl.pallas_call(
        functools.partial(reduce_kernel, cap=cap, rows=rows, lr=lr),
        out_shape=(jax.ShapeDtypeStruct((rows // 2 + rows // 2 // LANES, 2 * LANES), jnp.float32),) * 2,
        in_specs=[pl.BlockSpec(memory_space=pltpu.VMEM)] * 2,
        out_specs=(pl.BlockSpec(memory_space=pltpu.VMEM), pl.BlockSpec(memory_space=pltpu.VMEM)),
        scratch_shapes=[pltpu.VMEM((2 * cap, LANES), jnp.float32)]
        + [pltpu.VMEM((2 * rows + 8, LANES), jnp.float32)] * 4
        + [
            pltpu.VMEM((rows // 2 // LANES, LANES), jnp.float32),
            pltpu.VMEM((2 * recv.shape[0], LANES), jnp.int32),
            pltpu.SMEM((2 * recv.shape[0], LANES), jnp.int32),
            pltpu.SemaphoreType.DMA,
        ],
        compiler_params=pltpu.CompilerParams(vmem_limit_bytes=32 << 20),
        name="reduce",
    )(recv, acc2d)


LOG_STEPS = 340.0
FINE = 1.3e7
FULL = 32767.0


def put_log(x):
    return jnp.floor(jnp.log(jnp.maximum(x, 1e-18)) * (LOG_STEPS / 0.6931471805599453))


def get_log(code):
    return jnp.exp(code * (0.6931471805599453 / LOG_STEPS))


def put_pair(x):
    hi = put_log(x)
    lo = jnp.round((x / get_log(hi) - 1.0) * FINE)
    return hi, jnp.clip(lo, -FULL, FULL)


def get_pair(hi, lo):
    return get_log(hi) * (1.0 + lo * (1.0 / FINE))


def to_i16(x):
    return x.astype(jnp.int32).astype(jnp.int16)


def from_i16(x):
    return x.astype(jnp.int32).astype(jnp.float32)


def encode(ref, tail, j, t, ms_row):
    top = jnp.max(jnp.abs(t), axis=1, keepdims=True)
    top_b = jnp.broadcast_to(top, (LANES, LANES))
    code = put_log(top_b) + 2.0
    inv = FULL / get_log(code)
    ref[j * LANES : (j + 1) * LANES, 0:LANES] = to_i16(jnp.clip(jnp.round(t[:, :LANES] * inv), -FULL, FULL))
    ref[j * LANES : (j + 1) * LANES, LANES : 2 * LANES] = to_i16(
        jnp.clip(jnp.round(t[:, LANES:] * inv), -FULL, FULL)
    )
    hi, lo = put_pair(ms_row)
    tail[j : j + 1, 0:LANES] = jnp.transpose(code)[0:1, :]
    tail[j : j + 1, LANES : 2 * LANES] = hi
    tail[4 + j : 5 + j, 0:LANES] = lo


def decode(ref, tail, j):
    code = jnp.transpose(jnp.broadcast_to(tail[j : j + 1, 0:LANES], (LANES, LANES)))
    step = get_log(code) * (1.0 / FULL)
    lo = from_i16(ref[j * LANES : (j + 1) * LANES, 0:LANES]) * step
    hi = from_i16(ref[j * LANES : (j + 1) * LANES, LANES : 2 * LANES]) * step
    ms = get_pair(tail[j : j + 1, LANES : 2 * LANES], tail[4 + j : 5 + j, 0:LANES])
    return lo, hi, ms


def pair_kernel(keep_ref, recv_ref, own_ref, q1, q2, q3, tail, ms_v):
    chip = lax.axis_index("replica") // 2
    part = own_ref.shape[0] - 4
    blocks = part // LANES
    half = 4 * part
    tail[...] = jnp.zeros_like(tail)
    ms_at = slice(half, half + half // LANES)
    ms_v[...] = keep_ref[ms_at, 0:LANES] + recv_ref[ms_at, 0:LANES]
    for shift, ref in ((2, q2), (1, q1), (3, q3), (0, own_ref)):
        quarter = lax.rem(chip + shift, 4)
        for j in range(blocks):
            b = quarter * blocks + j
            r = pl.multiple_of(b * LANES, LANES)
            t = keep_ref[pl.ds(r, LANES), :] + recv_ref[pl.ds(r, LANES), :]
            ms = ms_v[pl.ds(b, 1), :]
            if shift:
                encode(ref, tail, j, t, ms)
            else:
                ref[j * LANES : (j + 1) * LANES, :] = t
                ref[part + j : part + j + 1, 0:LANES] = ms
        if shift:
            ref[part : part + 16, :] = to_i16(tail[...])


def pair_sum(keep, recv, part):
    coded = jax.ShapeDtypeStruct((part + 16, 2 * LANES), jnp.int16)
    return pl.pallas_call(
        pair_kernel,
        out_shape=(jax.ShapeDtypeStruct((part + 4, 2 * LANES), jnp.float32), coded, coded, coded),
        in_specs=[pl.BlockSpec(memory_space=pltpu.VMEM)] * 2,
        out_specs=(pl.BlockSpec(memory_space=pltpu.VMEM),) * 4,
        scratch_shapes=[
            pltpu.VMEM((16, 2 * LANES), jnp.float32),
            pltpu.VMEM((4 * part // LANES, LANES), jnp.float32),
        ],
        compiler_params=pltpu.CompilerParams(vmem_limit_bytes=12 << 20),
        name="pair_sum",
    )(keep, recv)


def chip_kernel(own_ref, r1, r2, r3, out_ref, tail, *, replicas):
    part = own_ref.shape[0] - 4
    tails = []
    for k, ref in enumerate((r1, r2, r3)):
        tail[16 * k : 16 * k + 16, :] = from_i16(ref[part : part + 16, :])
        tails.append(tail.at[16 * k : 16 * k + 16, :])
    last = tail.at[48:64, :]
    last[...] = jnp.zeros_like(last)
    for j in range(part // LANES):
        lo = own_ref[j * LANES : (j + 1) * LANES, 0:LANES]
        hi = own_ref[j * LANES : (j + 1) * LANES, LANES : 2 * LANES]
        ms = own_ref[part + j : part + j + 1, 0:LANES]
        for ref, t in zip((r1, r2, r3), tails):
            lo_k, hi_k, ms_k = decode(ref, t, j)
            lo, hi, ms = lo + lo_k, hi + hi_k, ms + ms_k
        both = jnp.concatenate([lo, hi], axis=1) * (1.0 / replicas)
        encode(out_ref, last, j, both, ms * (1.0 / replicas))
    out_ref[part : part + 16, :] = to_i16(last[...])


def chip_sum(own, r1, r2, r3, replicas):
    return pl.pallas_call(
        functools.partial(chip_kernel, replicas=replicas),
        out_shape=jax.ShapeDtypeStruct(r1.shape, jnp.int16),
        in_specs=[pl.BlockSpec(memory_space=pltpu.VMEM)] * 4,
        out_specs=pl.BlockSpec(memory_space=pltpu.VMEM),
        scratch_shapes=[pltpu.VMEM((64, 2 * LANES), jnp.float32)],
        compiler_params=pltpu.CompilerParams(vmem_limit_bytes=12 << 20),
        name="chip_sum",
    )(own, r1, r2, r3)


def update_kernel(emb_hbm, acc_ref, *refs, pieces):
    codes, (table_hbm, accum_ref, buf, tail, in_sems, out_sems) = refs[:pieces], refs[pieces:]
    part = buf.shape[1]
    blocks = part // LANES
    me = lax.axis_index("replica")
    chip, core = me // 2, lax.rem(me, 2)
    places = [
        (core if k < pieces // 2 else 1 - core) * (pieces // 2) + lax.rem(chip + pieces - k, pieces // 2)
        for k in range(pieces)
    ]
    spans = [pl.ds(pl.multiple_of(place * part, part), part) for place in places]
    loads = [pltpu.make_async_copy(emb_hbm.at[span], buf.at[k], in_sems.at[k]) for k, span in enumerate(spans)]
    stores = [pltpu.make_async_copy(buf.at[k], table_hbm.at[span], out_sems.at[k]) for k, span in enumerate(spans)]
    for load in loads:
        load.start()
    for k, ref in enumerate(codes):
        tail[...] = from_i16(ref[part : part + 16, :])
        loads[k].wait()
        for j in range(blocks):
            lo, hi, ms = decode(ref, tail, j)
            rows = slice(j * LANES, (j + 1) * LANES)
            buf[k, rows, 0:LANES] += lo
            buf[k, rows, LANES : 2 * LANES] += hi
            at = pl.ds(places[k] * blocks + j, 1)
            accum_ref[at, :] = acc_ref[at, :] + ms
        stores[k].start()
    for store in stores:
        store.wait()


def update(emb, acc2d, codes):
    part = codes[0].shape[0] - 16
    pieces = len(codes)
    return pl.pallas_call(
        functools.partial(update_kernel, pieces=pieces),
        out_shape=(jax.ShapeDtypeStruct(emb.shape, jnp.float32), jax.ShapeDtypeStruct(acc2d.shape, jnp.float32)),
        in_specs=[pl.BlockSpec(memory_space=pltpu.HBM)] + [pl.BlockSpec(memory_space=pltpu.VMEM)] * (1 + pieces),
        out_specs=(pl.BlockSpec(memory_space=pltpu.HBM), pl.BlockSpec(memory_space=pltpu.VMEM)),
        scratch_shapes=[
            pltpu.VMEM((pieces, part, 2 * LANES), jnp.float32),
            pltpu.VMEM((16, 2 * LANES), jnp.float32),
            pltpu.SemaphoreType.DMA((pieces,)),
            pltpu.SemaphoreType.DMA((pieces,)),
        ],
        compiler_params=pltpu.CompilerParams(vmem_limit_bytes=20 << 20),
        name="update",
    )(pltpu.with_memory_space_constraint(emb, pltpu.HBM), acc2d, *codes)


learn_rate = 0.5


def shards(emb_table, row_accum, row_grads, owner_ids, local_row):
    owners = lax.axis_size("mp")
    replicas = lax.axis_size("replica")
    n = row_grads.shape[0]
    rows = emb_table.shape[0]
    cap = 2 * n // owners
    own2d = owner_ids.reshape(n // LANES, LANES)
    row2d = local_row.reshape(n // LANES, LANES)
    acc2d = row_accum.reshape(rows // LANES, LANES)
    outgoing = pack(own2d, row2d, row_grads, owners, cap)
    incoming = lax.all_to_all(outgoing, "mp", split_axis=0, concat_axis=0, tiled=True)
    keep, send = reduce(incoming, acc2d, cap, learn_rate)

    def hop(v, chips):
        return lax.ppermute(v, "replica", [(k, (k + 2 * chips) % replicas) for k in range(replicas)])

    def swap(v):
        return lax.ppermute(v, "replica", [(k, k ^ 1) for k in range(replicas)])

    own, q1, q2, q3 = pair_sum(keep, swap(send), rows // replicas)
    mine = chip_sum(own, hop(q1, 1), hop(q2, 2), hop(q3, 3), replicas)
    here = [mine] + [hop(mine, s) for s in (1, 2, 3)]
    there = [swap(v) for v in here]
    table, accum = update(emb_table, acc2d, here + there)
    return table, accum.reshape(rows)


def solution(mesh):
    return jax.shard_map(
        shards,
        mesh=mesh,
        in_specs=(
            P("mp", None),
            P("mp"),
            P(("replica", "mp"), None),
            P(("replica", "mp"), None),
            P(("replica", "mp")),
        ),
        out_specs=(P("mp", None), P("mp")),
        check_vma=False,
    )
```

```python
import functools
import jax
import jax.numpy as jnp
from jax import lax
from jax.experimental import pallas as pl
from jax.experimental.pallas import tpu as pltpu
from jax.sharding import PartitionSpec as P

LANES = 128


def pack_kernel(
    owner_hbm, row_hbm, grads_hbm, out_ref, owner_ref, row_ref, grads_ref, x32, out32, slot_v, slot_s, sems, *, owners, cap, pad
):
    loads = [
        pltpu.make_async_copy(src, dst, sems.at[k])
        for k, (src, dst) in enumerate(((owner_hbm, owner_ref), (row_hbm, row_ref), (grads_hbm, grads_ref)))
    ]
    for load in loads:
        load.start()
    nb = owner_ref.shape[0]
    n = nb * LANES
    sub = lax.broadcasted_iota(jnp.int32, (owners, LANES), 0)
    upper = (lax.broadcasted_iota(jnp.int32, (LANES, LANES), 0)
             < lax.broadcasted_iota(jnp.int32, (LANES, LANES), 1)).astype(jnp.bfloat16)
    cap_iota = lax.broadcasted_iota(jnp.int32, (cap, LANES), 0)
    loads[0].wait()
    loads[1].wait()
    carry = jnp.zeros((owners, 1), jnp.float32)
    tgt = jnp.zeros((2 * owners, cap), jnp.float32)
    for b in range(nb):
        own = owner_ref[b:b + 1, :]
        hit = sub == jnp.broadcast_to(own, (owners, LANES))
        hot = hit.astype(jnp.float32)
        before = jnp.dot(hot.astype(jnp.bfloat16), upper, preferred_element_type=jnp.float32)
        pos = jnp.sum(jnp.where(hit, before + carry, 0.0), axis=0, keepdims=True).astype(jnp.int32)
        carry = carry + jnp.sum(hot, axis=1, keepdims=True)
        slot_v[b:b + 1, :] = 2 * (own * cap + pos)
        code = row_ref[b:b + 1, :] + 1
        hi = (code >> 6).astype(jnp.float32)
        lo = (code & 63).astype(jnp.float32)
        lhs = jnp.concatenate([hot * hi, hot * lo], axis=0).astype(jnp.bfloat16)
        rhs = (cap_iota == jnp.broadcast_to(pos, (cap, LANES))).astype(jnp.float32).astype(jnp.bfloat16)
        tgt = tgt + lax.dot_general(lhs, rhs, (((1,), (1,)), ((), ())), preferred_element_type=jnp.float32)
    copy = pltpu.make_async_copy(slot_v, slot_s, sems.at[3])
    copy.start()
    tb = tgt.astype(jnp.bfloat16)
    parts = [tb[:owners, :LANES], tb[:owners, LANES:], tb[owners:, :LANES], tb[owners:, LANES:]]
    parts += [jnp.zeros((owners, LANES), jnp.bfloat16)] * (pad - 4)
    for k in range(pad):
        x = parts[k]
        for o in range(owners):
            out_ref[o, 2 * cap + k:2 * cap + k + 1, :] = x[o:o + 1, :]

    blk = 128
    loads[2].wait()

    @pl.loop(0, n // blk)
    def _(b):
        r = pl.multiple_of(b * blk, blk)
        g = grads_ref[pl.ds(r, blk), :].astype(jnp.float32)
        x32[pl.ds(2 * r, blk, stride=2), :] = g[:, :LANES]
        x32[pl.ds(2 * r + 1, blk, stride=2), :] = g[:, LANES:]

    copy.wait()

    @pl.loop(0, nb)
    def _(b):
        for j in range(LANES):
            s = slot_s[b, j]
            out32[pl.ds(s, 2), :] = x32[pl.ds(2 * (b * LANES + j), 2), :]

    @pl.loop(0, owners)
    def _(o):
        out_ref[o, 0:2 * cap, :] = out32[pl.ds(pl.multiple_of(o * 2 * cap, 2 * cap), 2 * cap), :].astype(jnp.bfloat16)


def pack(owner, row, grads, owners, cap, pad=8):
    n = grads.shape[0]
    nb = n // LANES
    return pl.pallas_call(
        functools.partial(pack_kernel, owners=owners, cap=cap, pad=pad),
        out_shape=jax.ShapeDtypeStruct((owners, 2 * cap + pad, LANES), jnp.bfloat16),
        in_specs=[pl.BlockSpec(memory_space=pltpu.HBM)] * 3,
        out_specs=pl.BlockSpec(memory_space=pltpu.VMEM),
        scratch_shapes=[
            pltpu.VMEM((nb, LANES), jnp.int32),
            pltpu.VMEM((nb, LANES), jnp.int32),
            pltpu.VMEM((n, 2 * LANES), jnp.bfloat16),
            pltpu.VMEM((2 * n, LANES), jnp.float32),
            pltpu.VMEM((2 * owners * cap, LANES), jnp.float32),
            pltpu.VMEM((nb, LANES), jnp.int32),
            pltpu.SMEM((nb, LANES), jnp.int32),
            pltpu.SemaphoreType.DMA((4,)),
        ],
        compiler_params=pltpu.CompilerParams(vmem_limit_bytes=24 << 20),
        name="pack",
    )(*[pltpu.with_memory_space_constraint(x, pltpu.HBM) for x in (owner, row, grads)])


def reduce_kernel(recv_ref, acc_ref, keep_ref, send_ref, xbuf, a0, a1, a2, a3, a4, a5, ms_v, idx_v, idx_s, sem, *, cap, rows, lr):
    accs = [a0, a1, a2, a3, a4, a5]
    owners = recv_ref.shape[0]
    @pl.loop(0, owners)
    def _(o):
        t = recv_ref[o, 2 * cap:2 * cap + 8, :].astype(jnp.float32)
        code = (t[0:2] * 64.0 + t[2:4]).astype(jnp.int32)
        idx_v[pl.ds(2 * o, 2), :] = jnp.where(code == 0, 2 * rows, 2 * code - 2)
    copy = pltpu.make_async_copy(idx_v, idx_s, sem)
    copy.start()
    zb = 512
    @pl.loop(0, 2 * rows // zb)
    def _(b):
        for a in accs:
            a[pl.ds(pl.multiple_of(b * zb, zb), zb), :] = jnp.zeros((zb, LANES), jnp.float32)
    copy.wait()

    @pl.loop(0, owners)
    def _(o):
        xbuf[...] = recv_ref[o, 0:2 * cap, :].astype(jnp.float32)
        for h in range(2):
            for j in range(LANES):
                at = pl.ds(idx_s[2 * o + h, j], 2)
                accs[j % 6][at, :] += xbuf[2 * (h * LANES + j) : 2 * (h * LANES + j) + 2, :]

    core = lax.rem(lax.axis_index("replica"), 2)
    half = rows // 2
    for ref, which in ((send_ref, 1 - core), (keep_ref, core)):
        for b in range(half // LANES):
            block = which * (half // LANES) + b
            base = pl.multiple_of(block * 2 * LANES, 2 * LANES)
            lo, hi = [
                ((a0[at, :] + a1[at, :]) + (a2[at, :] + a3[at, :])) + (a4[at, :] + a5[at, :])
                for at in (pl.ds(base, LANES, stride=2), pl.ds(base + 1, LANES, stride=2))
            ]
            total = jnp.sum(lo * lo + hi * hi, axis=1, keepdims=True)
            ms = jnp.transpose(jnp.broadcast_to(total, (LANES, LANES)))[0:1, :] * (1.0 / (2 * LANES))
            ms_v[b : b + 1, :] = ms
            coef = -lr / jnp.sqrt(acc_ref[pl.ds(block, 1), :] + ms)
            coef = jnp.transpose(jnp.broadcast_to(coef, (LANES, LANES)))
            ref[b * LANES : (b + 1) * LANES, 0:LANES] = lo * coef
            ref[b * LANES : (b + 1) * LANES, LANES : 2 * LANES] = hi * coef

        ref[half : half + half // LANES, 0:LANES] = ms_v[...]


def reduce(recv, acc2d, cap, lr):
    rows = acc2d.size
    return pl.pallas_call(
        functools.partial(reduce_kernel, cap=cap, rows=rows, lr=lr),
        out_shape=(jax.ShapeDtypeStruct((rows // 2 + rows // 2 // LANES, 2 * LANES), jnp.float32),) * 2,
        in_specs=[pl.BlockSpec(memory_space=pltpu.VMEM)] * 2,
        out_specs=(pl.BlockSpec(memory_space=pltpu.VMEM), pl.BlockSpec(memory_space=pltpu.VMEM)),
        scratch_shapes=[pltpu.VMEM((2 * cap, LANES), jnp.float32)]
        + [pltpu.VMEM((2 * rows + 8, LANES), jnp.float32)] * 6
        + [
            pltpu.VMEM((rows // 2 // LANES, LANES), jnp.float32),
            pltpu.VMEM((2 * recv.shape[0], LANES), jnp.int32),
            pltpu.SMEM((2 * recv.shape[0], LANES), jnp.int32),
            pltpu.SemaphoreType.DMA,
        ],
        compiler_params=pltpu.CompilerParams(vmem_limit_bytes=42 << 20),
        name="reduce",
    )(recv, acc2d)


LOG_STEPS = 340.0
FINE = 1.3e7
FULL = 32767.0


def put_log(x):
    return jnp.floor(jnp.log(jnp.maximum(x, 1e-18)) * (LOG_STEPS / 0.6931471805599453))


def get_log(code):
    return jnp.exp(code * (0.6931471805599453 / LOG_STEPS))


def put_pair(x):
    hi = put_log(x)
    lo = jnp.round((x / get_log(hi) - 1.0) * FINE)
    return hi, jnp.clip(lo, -FULL, FULL)


def get_pair(hi, lo):
    return get_log(hi) * (1.0 + lo * (1.0 / FINE))


def to_i16(x):
    return x.astype(jnp.int32).astype(jnp.int16)


def from_i16(x):
    return x.astype(jnp.int32).astype(jnp.float32)


def encode(ref, tail, j, t, ms_row):
    top = jnp.max(jnp.abs(t), axis=1, keepdims=True)
    top_b = jnp.broadcast_to(top, (LANES, LANES))
    code = put_log(top_b) + 2.0
    inv = FULL / get_log(code)
    ref[j * LANES : (j + 1) * LANES, 0:LANES] = to_i16(jnp.clip(jnp.round(t[:, :LANES] * inv), -FULL, FULL))
    ref[j * LANES : (j + 1) * LANES, LANES : 2 * LANES] = to_i16(
        jnp.clip(jnp.round(t[:, LANES:] * inv), -FULL, FULL)
    )
    hi, lo = put_pair(ms_row)
    tail[j : j + 1, 0:LANES] = jnp.transpose(code)[0:1, :]
    tail[j : j + 1, LANES : 2 * LANES] = hi
    tail[4 + j : 5 + j, 0:LANES] = lo


def decode(ref, tail, j):
    code = jnp.transpose(jnp.broadcast_to(tail[j : j + 1, 0:LANES], (LANES, LANES)))
    step = get_log(code) * (1.0 / FULL)
    lo = from_i16(ref[j * LANES : (j + 1) * LANES, 0:LANES]) * step
    hi = from_i16(ref[j * LANES : (j + 1) * LANES, LANES : 2 * LANES]) * step
    ms = get_pair(tail[j : j + 1, LANES : 2 * LANES], tail[4 + j : 5 + j, 0:LANES])
    return lo, hi, ms


def pair_kernel(keep_ref, recv_ref, own_ref, q1, q2, q3, tail, ms_v):
    chip = lax.axis_index("replica") // 2
    part = own_ref.shape[0] - 4
    blocks = part // LANES
    half = 4 * part
    tail[...] = jnp.zeros_like(tail)
    ms_at = slice(half, half + half // LANES)
    ms_v[...] = keep_ref[ms_at, 0:LANES] + recv_ref[ms_at, 0:LANES]
    for shift, ref in ((2, q2), (1, q1), (3, q3), (0, own_ref)):
        quarter = lax.rem(chip + shift, 4)
        for j in range(blocks):
            b = quarter * blocks + j
            r = pl.multiple_of(b * LANES, LANES)
            t = keep_ref[pl.ds(r, LANES), :] + recv_ref[pl.ds(r, LANES), :]
            ms = ms_v[pl.ds(b, 1), :]
            if shift:
                encode(ref, tail, j, t, ms)
            else:
                ref[j * LANES : (j + 1) * LANES, :] = t
                ref[part + j : part + j + 1, 0:LANES] = ms
        if shift:
            ref[part : part + 16, :] = to_i16(tail[...])


def pair_sum(keep, recv, part):
    coded = jax.ShapeDtypeStruct((part + 16, 2 * LANES), jnp.int16)
    return pl.pallas_call(
        pair_kernel,
        out_shape=(jax.ShapeDtypeStruct((part + 4, 2 * LANES), jnp.float32), coded, coded, coded),
        in_specs=[pl.BlockSpec(memory_space=pltpu.VMEM)] * 2,
        out_specs=(pl.BlockSpec(memory_space=pltpu.VMEM),) * 4,
        scratch_shapes=[
            pltpu.VMEM((16, 2 * LANES), jnp.float32),
            pltpu.VMEM((4 * part // LANES, LANES), jnp.float32),
        ],
        compiler_params=pltpu.CompilerParams(vmem_limit_bytes=12 << 20),
        name="pair_sum",
    )(keep, recv)


def chip_kernel(own_ref, r1, r2, r3, out_ref, tail, *, replicas):
    part = own_ref.shape[0] - 4
    tails = []
    for k, ref in enumerate((r1, r2, r3)):
        tail[16 * k : 16 * k + 16, :] = from_i16(ref[part : part + 16, :])
        tails.append(tail.at[16 * k : 16 * k + 16, :])
    last = tail.at[48:64, :]
    last[...] = jnp.zeros_like(last)
    for j in range(part // LANES):
        lo = own_ref[j * LANES : (j + 1) * LANES, 0:LANES]
        hi = own_ref[j * LANES : (j + 1) * LANES, LANES : 2 * LANES]
        ms = own_ref[part + j : part + j + 1, 0:LANES]
        for ref, t in zip((r1, r2, r3), tails):
            lo_k, hi_k, ms_k = decode(ref, t, j)
            lo, hi, ms = lo + lo_k, hi + hi_k, ms + ms_k
        both = jnp.concatenate([lo, hi], axis=1) * (1.0 / replicas)
        encode(out_ref, last, j, both, ms * (1.0 / replicas))
    out_ref[part : part + 16, :] = to_i16(last[...])


def chip_sum(own, r1, r2, r3, replicas):
    return pl.pallas_call(
        functools.partial(chip_kernel, replicas=replicas),
        out_shape=jax.ShapeDtypeStruct(r1.shape, jnp.int16),
        in_specs=[pl.BlockSpec(memory_space=pltpu.VMEM)] * 4,
        out_specs=pl.BlockSpec(memory_space=pltpu.VMEM),
        scratch_shapes=[pltpu.VMEM((64, 2 * LANES), jnp.float32)],
        compiler_params=pltpu.CompilerParams(vmem_limit_bytes=12 << 20),
        name="chip_sum",
    )(own, r1, r2, r3)


def update_kernel(emb_hbm, acc_ref, *refs, pieces):
    codes, (table_hbm, accum_ref, buf, tail, in_sems, out_sems) = refs[:pieces], refs[pieces:]
    part = buf.shape[1]
    blocks = part // LANES
    me = lax.axis_index("replica")
    chip, core = me // 2, lax.rem(me, 2)
    places = [
        (core if k < pieces // 2 else 1 - core) * (pieces // 2) + lax.rem(chip + pieces - k, pieces // 2)
        for k in range(pieces)
    ]
    spans = [pl.ds(pl.multiple_of(place * part, part), part) for place in places]
    loads = [pltpu.make_async_copy(emb_hbm.at[span], buf.at[k], in_sems.at[k]) for k, span in enumerate(spans)]
    stores = [pltpu.make_async_copy(buf.at[k], table_hbm.at[span], out_sems.at[k]) for k, span in enumerate(spans)]
    for load in loads:
        load.start()
    for k, ref in enumerate(codes):
        tail[...] = from_i16(ref[part : part + 16, :])
        loads[k].wait()
        for j in range(blocks):
            lo, hi, ms = decode(ref, tail, j)
            rows = slice(j * LANES, (j + 1) * LANES)
            buf[k, rows, 0:LANES] += lo
            buf[k, rows, LANES : 2 * LANES] += hi
            at = pl.ds(places[k] * blocks + j, 1)
            accum_ref[at, :] = acc_ref[at, :] + ms
        stores[k].start()
    for store in stores:
        store.wait()


def update(emb, acc2d, codes):
    part = codes[0].shape[0] - 16
    pieces = len(codes)
    return pl.pallas_call(
        functools.partial(update_kernel, pieces=pieces),
        out_shape=(jax.ShapeDtypeStruct(emb.shape, jnp.float32), jax.ShapeDtypeStruct(acc2d.shape, jnp.float32)),
        in_specs=[pl.BlockSpec(memory_space=pltpu.HBM)] + [pl.BlockSpec(memory_space=pltpu.VMEM)] * (1 + pieces),
        out_specs=(pl.BlockSpec(memory_space=pltpu.HBM), pl.BlockSpec(memory_space=pltpu.VMEM)),
        scratch_shapes=[
            pltpu.VMEM((pieces, part, 2 * LANES), jnp.float32),
            pltpu.VMEM((16, 2 * LANES), jnp.float32),
            pltpu.SemaphoreType.DMA((pieces,)),
            pltpu.SemaphoreType.DMA((pieces,)),
        ],
        compiler_params=pltpu.CompilerParams(vmem_limit_bytes=20 << 20),
        name="update",
    )(pltpu.with_memory_space_constraint(emb, pltpu.HBM), acc2d, *codes)


learn_rate = 0.5


def shards(emb_table, row_accum, row_grads, owner_ids, local_row):
    owners = lax.axis_size("mp")
    replicas = lax.axis_size("replica")
    n = row_grads.shape[0]
    rows = emb_table.shape[0]
    cap = 2 * n // owners
    own2d = owner_ids.reshape(n // LANES, LANES)
    row2d = local_row.reshape(n // LANES, LANES)
    acc2d = row_accum.reshape(rows // LANES, LANES)
    outgoing = pack(own2d, row2d, row_grads, owners, cap)
    incoming = lax.all_to_all(outgoing, "mp", split_axis=0, concat_axis=0, tiled=True)
    keep, send = reduce(incoming, acc2d, cap, learn_rate)

    def hop(v, chips):
        return lax.ppermute(v, "replica", [(k, (k + 2 * chips) % replicas) for k in range(replicas)])

    def swap(v):
        return lax.ppermute(v, "replica", [(k, k ^ 1) for k in range(replicas)])

    own, q1, q2, q3 = pair_sum(keep, swap(send), rows // replicas)
    mine = chip_sum(own, hop(q1, 1), hop(q2, 2), hop(q3, 3), replicas)
    here = [mine] + [hop(mine, s) for s in (1, 2, 3)]
    there = [swap(v) for v in here]
    table, accum = update(emb_table, acc2d, here + there)
    return table, accum.reshape(rows)


def solution(mesh):
    return jax.shard_map(
        shards,
        mesh=mesh,
        in_specs=(
            P("mp", None),
            P("mp"),
            P(("replica", "mp"), None),
            P(("replica", "mp"), None),
            P(("replica", "mp")),
        ),
        out_specs=(P("mp", None), P("mp")),
        check_vma=False,
    )
```

```python
import functools
import jax
import jax.numpy as jnp
from jax import lax
from jax.experimental import pallas as pl
from jax.experimental.pallas import tpu as pltpu
from jax.sharding import PartitionSpec as P

LANES = 128


def pack_kernel(
    owner_hbm, row_hbm, grads_hbm, out_ref, owner_ref, row_ref, grads_ref, x32, out32, slot_v, slot_s, sems, *, owners, cap, pad
):
    loads = [
        pltpu.make_async_copy(src, dst, sems.at[k])
        for k, (src, dst) in enumerate(((owner_hbm, owner_ref), (row_hbm, row_ref), (grads_hbm, grads_ref)))
    ]
    for load in loads:
        load.start()
    nb = owner_ref.shape[0]
    n = nb * LANES
    sub = lax.broadcasted_iota(jnp.int32, (owners, LANES), 0)
    upper = (lax.broadcasted_iota(jnp.int32, (LANES, LANES), 0)
             < lax.broadcasted_iota(jnp.int32, (LANES, LANES), 1)).astype(jnp.bfloat16)
    cap_iota = lax.broadcasted_iota(jnp.int32, (cap, LANES), 0)
    loads[0].wait()
    loads[1].wait()
    carry = jnp.zeros((owners, 1), jnp.float32)
    tgt = jnp.zeros((2 * owners, cap), jnp.float32)
    for b in range(nb):
        own = owner_ref[b:b + 1, :]
        hit = sub == jnp.broadcast_to(own, (owners, LANES))
        hot = hit.astype(jnp.float32)
        before = jnp.dot(hot.astype(jnp.bfloat16), upper, preferred_element_type=jnp.float32)
        pos = jnp.sum(jnp.where(hit, before + carry, 0.0), axis=0, keepdims=True).astype(jnp.int32)
        carry = carry + jnp.sum(hot, axis=1, keepdims=True)
        slot_v[b:b + 1, :] = 2 * (own * cap + pos)
        code = row_ref[b:b + 1, :] + 1
        hi = (code >> 6).astype(jnp.float32)
        lo = (code & 63).astype(jnp.float32)
        lhs = jnp.concatenate([hot * hi, hot * lo], axis=0).astype(jnp.bfloat16)
        rhs = (cap_iota == jnp.broadcast_to(pos, (cap, LANES))).astype(jnp.float32).astype(jnp.bfloat16)
        tgt = tgt + lax.dot_general(lhs, rhs, (((1,), (1,)), ((), ())), preferred_element_type=jnp.float32)
    copy = pltpu.make_async_copy(slot_v, slot_s, sems.at[3])
    copy.start()
    tb = tgt.astype(jnp.bfloat16)
    parts = [tb[:owners, :LANES], tb[:owners, LANES:], tb[owners:, :LANES], tb[owners:, LANES:]]
    parts += [jnp.zeros((owners, LANES), jnp.bfloat16)] * (pad - 4)
    for k in range(pad):
        x = parts[k]
        for o in range(owners):
            out_ref[o, 2 * cap + k:2 * cap + k + 1, :] = x[o:o + 1, :]

    blk = 128
    loads[2].wait()

    @pl.loop(0, n // blk)
    def _(b):
        r = pl.multiple_of(b * blk, blk)
        g = grads_ref[pl.ds(r, blk), :].astype(jnp.float32)
        x32[pl.ds(2 * r, blk, stride=2), :] = g[:, :LANES]
        x32[pl.ds(2 * r + 1, blk, stride=2), :] = g[:, LANES:]

    copy.wait()

    @pl.loop(0, nb)
    def _(b):
        for j in range(LANES):
            s = slot_s[b, j]
            out32[pl.ds(s, 2), :] = x32[pl.ds(2 * (b * LANES + j), 2), :]

    @pl.loop(0, owners)
    def _(o):
        out_ref[o, 0:2 * cap, :] = out32[pl.ds(pl.multiple_of(o * 2 * cap, 2 * cap), 2 * cap), :].astype(jnp.bfloat16)


def pack(owner, row, grads, owners, cap, pad=8):
    n = grads.shape[0]
    nb = n // LANES
    return pl.pallas_call(
        functools.partial(pack_kernel, owners=owners, cap=cap, pad=pad),
        out_shape=jax.ShapeDtypeStruct((owners, 2 * cap + pad, LANES), jnp.bfloat16),
        in_specs=[pl.BlockSpec(memory_space=pltpu.HBM)] * 3,
        out_specs=pl.BlockSpec(memory_space=pltpu.VMEM),
        scratch_shapes=[
            pltpu.VMEM((nb, LANES), jnp.int32),
            pltpu.VMEM((nb, LANES), jnp.int32),
            pltpu.VMEM((n, 2 * LANES), jnp.bfloat16),
            pltpu.VMEM((2 * n, LANES), jnp.float32),
            pltpu.VMEM((2 * owners * cap, LANES), jnp.float32),
            pltpu.VMEM((nb, LANES), jnp.int32),
            pltpu.SMEM((nb, LANES), jnp.int32),
            pltpu.SemaphoreType.DMA((4,)),
        ],
        compiler_params=pltpu.CompilerParams(vmem_limit_bytes=24 << 20),
        name="pack",
    )(*[pltpu.with_memory_space_constraint(x, pltpu.HBM) for x in (owner, row, grads)])


def reduce_kernel(recv_ref, acc_ref, keep_ref, send_ref, xbuf, a0, a1, a2, a3, a4, a5, ms_v, idx_v, idx_s, sem, *, cap, rows, lr):
    accs = [a0, a1, a2, a3, a4, a5]
    owners = recv_ref.shape[0]
    @pl.loop(0, owners)
    def _(o):
        t = recv_ref[o, 2 * cap:2 * cap + 8, :].astype(jnp.float32)
        code = (t[0:2] * 64.0 + t[2:4]).astype(jnp.int32)
        idx_v[pl.ds(2 * o, 2), :] = jnp.where(code == 0, 2 * rows, 2 * code - 2)
    copy = pltpu.make_async_copy(idx_v, idx_s, sem)
    copy.start()
    zb = 512
    @pl.loop(0, 2 * rows // zb)
    def _(b):
        for a in accs:
            a[pl.ds(pl.multiple_of(b * zb, zb), zb), :] = jnp.zeros((zb, LANES), jnp.float32)
    copy.wait()

    @pl.loop(0, owners)
    def _(o):
        xbuf[...] = recv_ref[o, 0:2 * cap, :].astype(jnp.float32)
        for h in range(2):
            for j in range(LANES):
                at = pl.ds(idx_s[2 * o + h, j], 2)
                accs[j % 6][at, :] += xbuf[2 * (h * LANES + j) : 2 * (h * LANES + j) + 2, :]

    core = lax.rem(lax.axis_index("replica"), 2)
    half = rows // 2
    for ref, which in ((send_ref, 1 - core), (keep_ref, core)):
        for b in range(half // LANES):
            block = which * (half // LANES) + b
            base = pl.multiple_of(block * 2 * LANES, 2 * LANES)
            lo, hi = [
                ((a0[at, :] + a1[at, :]) + (a2[at, :] + a3[at, :])) + (a4[at, :] + a5[at, :])
                for at in (pl.ds(base, LANES, stride=2), pl.ds(base + 1, LANES, stride=2))
            ]
            total = jnp.sum(lo * lo + hi * hi, axis=1, keepdims=True)
            ms = jnp.transpose(jnp.broadcast_to(total, (LANES, LANES)))[0:1, :] * (1.0 / (2 * LANES))
            ms_v[b : b + 1, :] = ms
            coef = -lr / jnp.sqrt(acc_ref[pl.ds(block, 1), :] + ms)
            coef = jnp.transpose(jnp.broadcast_to(coef, (LANES, LANES)))
            ref[b * LANES : (b + 1) * LANES, 0:LANES] = lo * coef
            ref[b * LANES : (b + 1) * LANES, LANES : 2 * LANES] = hi * coef

        ref[half : half + half // LANES, 0:LANES] = ms_v[...]


def reduce(recv, acc2d, cap, lr):
    rows = acc2d.size
    return pl.pallas_call(
        functools.partial(reduce_kernel, cap=cap, rows=rows, lr=lr),
        out_shape=(jax.ShapeDtypeStruct((rows // 2 + rows // 2 // LANES, 2 * LANES), jnp.float32),) * 2,
        in_specs=[pl.BlockSpec(memory_space=pltpu.VMEM)] * 2,
        out_specs=(pl.BlockSpec(memory_space=pltpu.VMEM), pl.BlockSpec(memory_space=pltpu.VMEM)),
        scratch_shapes=[pltpu.VMEM((2 * cap, LANES), jnp.float32)]
        + [pltpu.VMEM((2 * rows + 8, LANES), jnp.float32)] * 6
        + [
            pltpu.VMEM((rows // 2 // LANES, LANES), jnp.float32),
            pltpu.VMEM((2 * recv.shape[0], LANES), jnp.int32),
            pltpu.SMEM((2 * recv.shape[0], LANES), jnp.int32),
            pltpu.SemaphoreType.DMA,
        ],
        compiler_params=pltpu.CompilerParams(vmem_limit_bytes=42 << 20),
        name="reduce",
    )(recv, acc2d)


LOG_STEPS = 340.0
FINE = 1.3e7
FULL = 32767.0


def put_log(x):
    return jnp.floor(jnp.log(jnp.maximum(x, 1e-18)) * (LOG_STEPS / 0.6931471805599453))


def get_log(code):
    return jnp.exp(code * (0.6931471805599453 / LOG_STEPS))


def put_pair(x):
    hi = put_log(x)
    lo = jnp.round((x / get_log(hi) - 1.0) * FINE)
    return hi, jnp.clip(lo, -FULL, FULL)


def get_pair(hi, lo):
    return get_log(hi) * (1.0 + lo * (1.0 / FINE))


def to_i16(x):
    return x.astype(jnp.int32).astype(jnp.int16)


def from_i16(x):
    return x.astype(jnp.int32).astype(jnp.float32)


def encode(ref, tail, j, t, ms_row):
    top = jnp.max(jnp.abs(t), axis=1, keepdims=True)
    top_b = jnp.broadcast_to(top, (LANES, LANES))
    code = put_log(top_b) + 2.0
    inv = FULL / get_log(code)
    ref[j * LANES : (j + 1) * LANES, 0:LANES] = to_i16(jnp.clip(jnp.round(t[:, :LANES] * inv), -FULL, FULL))
    ref[j * LANES : (j + 1) * LANES, LANES : 2 * LANES] = to_i16(
        jnp.clip(jnp.round(t[:, LANES:] * inv), -FULL, FULL)
    )
    hi, lo = put_pair(ms_row)
    tail[j : j + 1, 0:LANES] = jnp.transpose(code)[0:1, :]
    tail[j : j + 1, LANES : 2 * LANES] = hi
    tail[4 + j : 5 + j, 0:LANES] = lo


def decode(ref, tail, j):
    code = jnp.transpose(jnp.broadcast_to(tail[j : j + 1, 0:LANES], (LANES, LANES)))
    step = get_log(code) * (1.0 / FULL)
    lo = from_i16(ref[j * LANES : (j + 1) * LANES, 0:LANES]) * step
    hi = from_i16(ref[j * LANES : (j + 1) * LANES, LANES : 2 * LANES]) * step
    ms = get_pair(tail[j : j + 1, LANES : 2 * LANES], tail[4 + j : 5 + j, 0:LANES])
    return lo, hi, ms


def pair_kernel(keep_ref, recv_ref, own_ref, q1, q2, q3, tail, ms_v):
    chip = lax.axis_index("replica") // 2
    part = own_ref.shape[0] - 4
    blocks = part // LANES
    half = 4 * part
    tail[...] = jnp.zeros_like(tail)
    ms_at = slice(half, half + half // LANES)
    ms_v[...] = keep_ref[ms_at, 0:LANES] + recv_ref[ms_at, 0:LANES]
    for shift, ref in ((2, q2), (1, q1), (3, q3), (0, own_ref)):
        quarter = lax.rem(chip + shift, 4)
        for j in range(blocks):
            b = quarter * blocks + j
            r = pl.multiple_of(b * LANES, LANES)
            t = keep_ref[pl.ds(r, LANES), :] + recv_ref[pl.ds(r, LANES), :]
            ms = ms_v[pl.ds(b, 1), :]
            if shift:
                encode(ref, tail, j, t, ms)
            else:
                ref[j * LANES : (j + 1) * LANES, :] = t
                ref[part + j : part + j + 1, 0:LANES] = ms
        if shift:
            ref[part : part + 16, :] = to_i16(tail[...])


def pair_sum(keep, recv, part):
    coded = jax.ShapeDtypeStruct((part + 16, 2 * LANES), jnp.int16)
    return pl.pallas_call(
        pair_kernel,
        out_shape=(jax.ShapeDtypeStruct((part + 4, 2 * LANES), jnp.float32), coded, coded, coded),
        in_specs=[pl.BlockSpec(memory_space=pltpu.VMEM)] * 2,
        out_specs=(pl.BlockSpec(memory_space=pltpu.VMEM),) * 4,
        scratch_shapes=[
            pltpu.VMEM((16, 2 * LANES), jnp.float32),
            pltpu.VMEM((4 * part // LANES, LANES), jnp.float32),
        ],
        compiler_params=pltpu.CompilerParams(vmem_limit_bytes=12 << 20),
        name="pair_sum",
    )(keep, recv)


def chip_kernel(own_ref, r1, r2, r3, out_ref, tail, *, replicas):
    part = own_ref.shape[0] - 4
    tails = []
    for k, ref in enumerate((r1, r2, r3)):
        tail[16 * k : 16 * k + 16, :] = from_i16(ref[part : part + 16, :])
        tails.append(tail.at[16 * k : 16 * k + 16, :])
    last = tail.at[48:64, :]
    last[...] = jnp.zeros_like(last)
    for j in range(part // LANES):
        lo = own_ref[j * LANES : (j + 1) * LANES, 0:LANES]
        hi = own_ref[j * LANES : (j + 1) * LANES, LANES : 2 * LANES]
        ms = own_ref[part + j : part + j + 1, 0:LANES]
        for ref, t in zip((r1, r2, r3), tails):
            lo_k, hi_k, ms_k = decode(ref, t, j)
            lo, hi, ms = lo + lo_k, hi + hi_k, ms + ms_k
        both = jnp.concatenate([lo, hi], axis=1) * (1.0 / replicas)
        encode(out_ref, last, j, both, ms * (1.0 / replicas))
    out_ref[part : part + 16, :] = to_i16(last[...])


def chip_sum(own, r1, r2, r3, replicas):
    return pl.pallas_call(
        functools.partial(chip_kernel, replicas=replicas),
        out_shape=jax.ShapeDtypeStruct(r1.shape, jnp.int16),
        in_specs=[pl.BlockSpec(memory_space=pltpu.VMEM)] * 4,
        out_specs=pl.BlockSpec(memory_space=pltpu.VMEM),
        scratch_shapes=[pltpu.VMEM((64, 2 * LANES), jnp.float32)],
        compiler_params=pltpu.CompilerParams(vmem_limit_bytes=12 << 20),
        name="chip_sum",
    )(own, r1, r2, r3)


def update_kernel(emb_ref, acc_ref, *refs, pieces):
    codes, (table_hbm, accum_ref, buf, tail, out_sems) = refs[:pieces], refs[pieces:]
    part = buf.shape[1]
    blocks = part // LANES
    me = lax.axis_index("replica")
    chip, core = me // 2, lax.rem(me, 2)
    places = [
        (core if k < pieces // 2 else 1 - core) * (pieces // 2) + lax.rem(chip + pieces - k, pieces // 2)
        for k in range(pieces)
    ]
    spans = [pl.ds(pl.multiple_of(place * part, part), part) for place in places]
    stores = [pltpu.make_async_copy(buf.at[k], table_hbm.at[span], out_sems.at[k]) for k, span in enumerate(spans)]
    for k, ref in enumerate(codes):
        tail[...] = from_i16(ref[part : part + 16, :])
        for j in range(blocks):
            lo, hi, ms = decode(ref, tail, j)
            rows = slice(j * LANES, (j + 1) * LANES)
            from_row = pl.ds(pl.multiple_of(places[k] * part + j * LANES, LANES), LANES)
            buf[k, rows, 0:LANES] = emb_ref[from_row, 0:LANES] + lo
            buf[k, rows, LANES : 2 * LANES] = emb_ref[from_row, LANES : 2 * LANES] + hi
            at = pl.ds(places[k] * blocks + j, 1)
            accum_ref[at, :] = acc_ref[at, :] + ms
        stores[k].start()
    for store in stores:
        store.wait()


def update(emb, acc2d, codes):
    part = codes[0].shape[0] - 16
    pieces = len(codes)
    return pl.pallas_call(
        functools.partial(update_kernel, pieces=pieces),
        out_shape=(jax.ShapeDtypeStruct(emb.shape, jnp.float32), jax.ShapeDtypeStruct(acc2d.shape, jnp.float32)),
        in_specs=[pl.BlockSpec(memory_space=pltpu.VMEM)] * (2 + pieces),
        out_specs=(pl.BlockSpec(memory_space=pltpu.HBM), pl.BlockSpec(memory_space=pltpu.VMEM)),
        scratch_shapes=[
            pltpu.VMEM((pieces, part, 2 * LANES), jnp.float32),
            pltpu.VMEM((16, 2 * LANES), jnp.float32),
            pltpu.SemaphoreType.DMA((pieces,)),
        ],
        compiler_params=pltpu.CompilerParams(vmem_limit_bytes=20 << 20),
        name="update",
    )(emb, acc2d, *codes)


learn_rate = 0.5


def shards(emb_table, row_accum, row_grads, owner_ids, local_row):
    owners = lax.axis_size("mp")
    replicas = lax.axis_size("replica")
    n = row_grads.shape[0]
    rows = emb_table.shape[0]
    cap = 2 * n // owners
    own2d = owner_ids.reshape(n // LANES, LANES)
    row2d = local_row.reshape(n // LANES, LANES)
    acc2d = row_accum.reshape(rows // LANES, LANES)
    outgoing = pack(own2d, row2d, row_grads, owners, cap)
    incoming = lax.all_to_all(outgoing, "mp", split_axis=0, concat_axis=0, tiled=True)
    keep, send = reduce(incoming, acc2d, cap, learn_rate)

    def hop(v, chips):
        return lax.ppermute(v, "replica", [(k, (k + 2 * chips) % replicas) for k in range(replicas)])

    def swap(v):
        return lax.ppermute(v, "replica", [(k, k ^ 1) for k in range(replicas)])

    own, q1, q2, q3 = pair_sum(keep, swap(send), rows // replicas)
    mine = chip_sum(own, hop(q1, 1), hop(q2, 2), hop(q3, 3), replicas)
    here = [mine] + [hop(mine, s) for s in (1, 2, 3)]
    there = [swap(v) for v in here]
    table, accum = update(emb_table, acc2d, here + there)
    return table, accum.reshape(rows)


def solution(mesh):
    return jax.shard_map(
        shards,
        mesh=mesh,
        in_specs=(
            P("mp", None),
            P("mp"),
            P(("replica", "mp"), None),
            P(("replica", "mp"), None),
            P(("replica", "mp")),
        ),
        out_specs=(P("mp", None), P("mp")),
        check_vma=False,
    )
```
